32 devices in a mesh: gx: 8 (over z, y), gy: 4 (over x, core).
Axes of the slice: x: 2, y: 2, z: 4, core: 2. Of those that a mesh axis runs over, the one named last changes fastest.
Arguments:
- point_feats: bfloat16 [32, 262144], P(None, ('gx', 'gy')), may hold values from -1 to 1
- point_targets: bfloat16 [262144], P(('gx', 'gy')), may hold values from -6 to 6
- point_lists: int32 [32768, 8], P(('gx', 'gy')), may hold values from -1 to 8191, as said below
- brick_adjacency: int32 [1024, 4], P(('gx', 'gy')), may hold values from -1 to 1023, as said below
- voxel_feats: float32 [1024, 32, 512], P(('gx', 'gy')), may hold values from -0.25 to 0.25
- voxel_reg: float32 [1024, 512], P(('gx', 'gy')), may hold values from 0.25 to 2
Outputs:
- solution: float32 [1024, 512], P(('gx', 'gy'))
- residual: float32 [1024, 512], P(('gx', 'gy'))
The draws below stay inside these ranges and needn't reach their ends.
Inputs may be any that keep to these rules, and one draw needn't show every extreme that they name: `point_lists`: row s * 1024 + b lists, in its first slots, distinct indices of the points of source device s in brick b, all within that device's rows b * 8 to b * 8 + 7, then -1 in the remaining slots. Point rows named by no list are unused. `brick_adjacency`: entry k of brick b is the lattice neighbour of b in direction k (minus along the road, plus along the road, minus across, plus across) or -1; the relation is symmetric and -1 wherever the neighbour lies outside the lattice.
All inputs are finite; a program needn't handle non-finite values.
Results may differ from the reference program's by a relative error of at most 0.0003.
Values may be sent and summed in bfloat16 or wider, within the bound.
A program may use at most 64 MiB of HBM per device.

```python
import math
import jax
import jax.numpy as jnp
from jax import lax

FEAT = 32
VOX = 512
BX = 8
BY = 4
CAPB = 8
ITERS = 3
BR_DEV = 32
NB = 1024
P_DEV = 8192
POINTS = 262144
LX = 64
LY = 16
N_GX = 8
N_GY = 4
DEVICES = 32


def draw_point_lists(key, part):
    devices = NB // BR_DEV
    key_counts, key_own, key_shared, key_perm = jax.random.split(jax.random.fold_in(key, 11), 4)
    owner = jnp.arange(NB, dtype=jnp.int32) // BR_DEV
    hottest = 4 + 20 * owner // max(devices - 1, 1)
    raw = jax.random.randint(key_counts, (devices, NB), 0, 1 << 20) % hottest[None, :]
    counts = jnp.minimum(raw, CAPB)
    own_pick = jax.random.randint(key_own, (devices,), 0, NB)
    counts = counts.at[jnp.arange(devices), own_pick].set(CAPB)
    shared = jax.random.randint(key_shared, (), 0, NB)
    counts = counts.at[:, shared].set(CAPB)
    counts = counts.at[:, NB - 1].set(CAPB)
    slot = jnp.arange(CAPB, dtype=jnp.int32)
    scores = jax.random.randint(key_perm, (devices, NB, CAPB), 0, 1 << 20) * CAPB + slot[None, None, :]
    order = jnp.argsort(scores, axis=-1).astype(jnp.int32)
    brick = jnp.arange(NB, dtype=jnp.int32)[None, :, None]
    listed = jnp.where(slot[None, None, :] < counts[:, :, None], brick * CAPB + order, -1)
    return listed.reshape(devices * NB, CAPB).astype(jnp.int32)


def draw_brick_adjacency(key, part):
    key_x, key_y = jax.random.split(jax.random.fold_in(key, 7))
    keep_x = jax.random.randint(key_x, (LX - 1, LY), 0, 4) > 0
    keep_y = jax.random.randint(key_y, (LX, LY - 1), 0, 4) > 0
    place_x = jnp.arange(LX, dtype=jnp.int32)[:, None]
    place_y = jnp.arange(LY, dtype=jnp.int32)[None, :]
    ident = (place_x // BX * (LY // BY) + place_y // BY) * BR_DEV + place_x % BX * BY + place_y % BY
    minus_x = jnp.where(jnp.pad(keep_x, ((1, 0), (0, 0))), jnp.pad(ident[:-1], ((1, 0), (0, 0))), -1)
    plus_x = jnp.where(jnp.pad(keep_x, ((0, 1), (0, 0))), jnp.pad(ident[1:], ((0, 1), (0, 0))), -1)
    minus_y = jnp.where(jnp.pad(keep_y, ((0, 0), (1, 0))), jnp.pad(ident[:, :-1], ((0, 0), (1, 0))), -1)
    plus_y = jnp.where(jnp.pad(keep_y, ((0, 0), (0, 1))), jnp.pad(ident[:, 1:], ((0, 0), (0, 1))), -1)
    lattice = jnp.stack([minus_x, plus_x, minus_y, plus_y], axis=-1)
    shaped = lattice.reshape(LX // BX, BX, LY // BY, BY, 4).transpose(0, 2, 1, 3, 4)
    return shaped.reshape(NB, 4).astype(jnp.int32)


def shard_levels(rng, extent, cuts, low, high):
    level = 1.0
    for position, parts in cuts:
        draws = jax.random.uniform(jax.random.fold_in(jax.random.fold_in(rng, 6), position), (parts,), jnp.float32, low / len(cuts), high / len(cuts))
        level = level * jnp.repeat(jnp.exp(draws), extent[position] // parts).reshape((-1,) + (1,) * (len(extent) - 1 - position))
    return level


def scatter_about(rng, extent, scale, limit, cuts=(), held_as=jnp.bfloat16):
    values = scale * jax.random.normal(rng, extent, jnp.float32)
    if cuts:
        values = values * shard_levels(rng, extent, cuts, -0.22, 0.18)
    return jnp.clip(values, -limit, limit).astype(held_as)


def setup_inputs(seed: int = 0) -> dict:
    arg_keys = jax.random.split(jax.random.key(seed), 7)
    return {
        "point_feats": scatter_about(arg_keys[0], (FEAT, POINTS), (DEVICES ** -0.5), 1.0, ((1, 32),)),
        "point_targets": scatter_about(arg_keys[1], (POINTS,), 1.0, 6.0, ((0, 32),)),
        "point_lists": draw_point_lists(jax.random.fold_in(arg_keys[6], 71), 0),
        "brick_adjacency": draw_brick_adjacency(jax.random.fold_in(arg_keys[6], 71), 0),
        "voxel_feats": scatter_about(arg_keys[4], (NB, FEAT, VOX), VOX ** -0.5, 0.25, ((0, 32),), jnp.float32),
        "voxel_reg": jnp.clip(jnp.exp(math.log(2.0) - 2.0794415 * jax.random.uniform(arg_keys[5], (NB, VOX), jnp.float32) ** shard_levels(arg_keys[5], (NB, VOX), ((0, 32),), -0.2, 0.2)), 0.25, 2.0),
    }


coupling_weight = 1.0


def to_lattice(values):
    width = values.shape[-1]
    shaped = values.reshape(N_GX, N_GY, BX, BY, width).transpose(0, 2, 1, 3, 4)
    return shaped.reshape(BX * N_GX, BY * N_GY, width)


def from_lattice(values):
    width = values.shape[-1]
    shaped = values.reshape(N_GX, BX, N_GY, BY, width).transpose(0, 2, 1, 3, 4)
    return shaped.reshape(BR_DEV * N_GX * N_GY, width)


def neighbour_sum(lattice, mask):
    padded = jnp.pad(lattice, ((1, 1), (1, 1), (0, 0)))
    total = mask[..., 0:1] * padded[:-2, 1:-1] + mask[..., 1:2] * padded[2:, 1:-1]
    return total + mask[..., 2:3] * padded[1:-1, :-2] + mask[..., 3:4] * padded[1:-1, 2:]


def reference(point_feats, point_targets, point_lists, brick_adjacency, voxel_feats, voxel_reg):
    devices = N_GX * N_GY
    lists = point_lists.reshape(devices, NB, CAPB)
    base = (jnp.arange(devices, dtype=jnp.int32) * P_DEV)[:, None, None]

    def one_owner(owner):
        rows = lax.dynamic_slice_in_dim(lists, (owner * BR_DEV).astype(jnp.int32), BR_DEV, 1)
        live = rows >= 0
        index = (jnp.where(live, rows, 0) + base).reshape(-1)
        feats = jnp.take(point_feats, index, axis=1).astype(jnp.float32).reshape(FEAT, devices, BR_DEV, CAPB)
        feats = jnp.where(live[None], feats, jnp.zeros((), jnp.float32))
        target = jnp.take(point_targets, index).astype(jnp.float32).reshape(live.shape)
        target = jnp.where(live, target, jnp.zeros((), jnp.float32))
        moment = jnp.einsum("isbc,jsbc->bij", feats, feats, precision=lax.Precision.HIGHEST)
        gathered = jnp.einsum("sbc,isbc->bi", target, feats, precision=lax.Precision.HIGHEST)
        return moment, gathered

    moments, gathered = lax.map(one_owner, jnp.arange(devices, dtype=jnp.int32))
    moments = moments.reshape(NB, FEAT, FEAT)
    gathered = gathered.reshape(NB, FEAT)
    mask = to_lattice((brick_adjacency >= 0).astype(jnp.float32))
    degree = jnp.sum(mask, axis=-1, keepdims=True)

    def operate(vector):
        projected = jnp.einsum("bik,bk->bi", voxel_feats, vector, precision=lax.Precision.HIGHEST)
        lattice = to_lattice(projected)
        coupled = from_lattice(degree * lattice - neighbour_sum(lattice, mask))
        middle = jnp.einsum("bij,bj->bi", moments, projected, precision=lax.Precision.HIGHEST)
        middle = middle + coupling_weight * coupled
        back = jnp.einsum("bik,bi->bk", voxel_feats, middle, precision=lax.Precision.HIGHEST)
        return back + voxel_reg * vector

    rhs = jnp.einsum("bik,bi->bk", voxel_feats, gathered, precision=lax.Precision.HIGHEST)
    solution = jnp.zeros_like(rhs)
    residual, direction = rhs, rhs
    norm_now = jnp.sum(residual * residual)
    for iteration in range(ITERS):
        image = operate(direction)
        alpha = norm_now / jnp.sum(direction * image)
        solution = solution + alpha * direction
        residual = residual - alpha * image
        norm_next = jnp.sum(residual * residual)
        direction = residual + (norm_next / norm_now) * direction
        norm_now = norm_next
    return solution, residual
```

```python
import functools

import jax
import jax.numpy as jnp
from jax import lax
from jax.experimental import pallas as pl
from jax.experimental.pallas import tpu as pltpu
from jax.sharding import PartitionSpec as P

BX = 8
BY = 4
ITERS = 3
LANES = 128
CHUNK = 8
MESH = pl.DeviceIdType.MESH

coupling_weight = 1.0


def kernel(
    gx,
    gy,
    feats_hbm,
    extra_hbm,
    adjacency_ref,
    voxel_hbm,
    reg_ref,
    solution_ref,
    residual_ref,
    got,
    got_extra,
    voxel,
    acc,
    vec,
    image,
    direction,
    carried,
    z_ref,
    my_ref,
    mid_ref,
    ym_ref,
    yp_ref,
    y_send,
    halo,
    part,
    parts,
    voxel_sem,
    feat_send,
    feat_recv,
    extra_send,
    extra_recv,
    halo_send,
    halo_recv,
    part_send,
    part_recv,
):
    count = gx * gy
    ix, iy = lax.axis_index("gx"), lax.axis_index("gy")
    me = ix * gy + iy
    feat, cols = got.shape[1], got.shape[2]
    bricks = vec.shape[0]
    slots = cols // bricks
    halves = cols // LANES
    per_half = LANES // slots

    def place(index):
        return (index // gy, index % gy)

    barrier = pltpu.get_barrier_semaphore()

    def greet(j, _):
        pl.semaphore_signal(
            barrier, inc=1, device_id=place((me + j) % count), device_id_type=MESH
        )
        return 0

    lax.fori_loop(1, count, greet, 0)
    voxel_copy = pltpu.make_async_copy(voxel_hbm, voxel, voxel_sem)
    voxel_copy.start()
    halo[...] = jnp.zeros_like(halo)
    acc[...] = jnp.zeros_like(acc)
    own_feat = pltpu.make_async_copy(
        feats_hbm.at[:, pl.ds(pl.multiple_of(me * cols, cols), cols)], got.at[me], feat_recv.at[me]
    )
    own_extra = pltpu.make_async_copy(extra_hbm.at[me], got_extra.at[me], extra_recv.at[me])
    own_feat.start()
    own_extra.start()
    pl.semaphore_wait(barrier, count - 1)

    def feat_copy(to, frm):
        return pltpu.make_async_remote_copy(
            src_ref=feats_hbm.at[:, pl.ds(pl.multiple_of(to * cols, cols), cols)],
            dst_ref=got.at[frm],
            send_sem=feat_send.at[to],
            recv_sem=feat_recv.at[frm],
            device_id=place(to),
            device_id_type=MESH,
        )

    def extra_copy(to, frm):
        return pltpu.make_async_remote_copy(
            src_ref=extra_hbm.at[to],
            dst_ref=got_extra.at[frm],
            send_sem=extra_send.at[to],
            recv_sem=extra_recv.at[frm],
            device_id=place(to),
            device_id_type=MESH,
        )

    def send(j, _):
        to = (me + j) % count
        feat_copy(to, me).start()
        extra_copy(to, me).start()
        return 0

    lax.fori_loop(1, count, send, 0)
    own_feat.wait()
    own_extra.wait()

    group = 4
    while count % group:
        group //= 2
    lane = lax.broadcasted_iota(jnp.int32, (1, group * LANES), 1)
    owner = (lane // slots) % per_half

    def absorb(g, _):
        sources = []
        for u in range(group):
            j = g * group + u
            source = (me + count - j) % count
            sources.append(source)
            if u:
                feat_copy(source, source).wait_recv()
                extra_copy(source, source).wait_recv()
            else:

                @pl.when(g > 0)
                def _():
                    feat_copy(source, source).wait_recv()
                    extra_copy(source, source).wait_recv()

        for h in range(halves):
            span = slice(h * LANES, (h + 1) * LANES)
            x = jnp.concatenate([got[s, :, span] for s in sources], axis=1)
            extra = jnp.concatenate(
                [got_extra[s, :, span].astype(jnp.float32) for s in sources], axis=1
            )
            live = extra[0:1]
            target = extra[1:2].astype(jnp.bfloat16)
            left = jnp.concatenate(
                [x * jnp.where(owner == b, live, 0.0).astype(jnp.bfloat16) for b in range(per_half)],
                axis=0,
            )
            right = jnp.concatenate(
                [
                    x,
                    jnp.broadcast_to(target, (16, group * LANES)),
                    jnp.zeros((LANES - feat - 16, group * LANES), jnp.bfloat16),
                ],
                axis=0,
            )
            rows = slice(h * per_half * feat, (h + 1) * per_half * feat)
            acc[rows, :] += lax.dot_general(
                left, right, (((1,), (1,)), ((), ())), preferred_element_type=jnp.float32
            )
        return 0

    lax.fori_loop(0, count // group, absorb, 0)
    voxel_copy.wait()

    eye = lax.broadcasted_iota(jnp.int32, (1, feat, LANES), 1) == lax.broadcasted_iota(
        jnp.int32, (1, feat, LANES), 2
    )
    chunks = bricks // CHUNK

    def at(t):
        return pl.ds(pl.multiple_of(t * CHUNK, CHUNK), CHUNK)

    def moment_at(t):
        rows = pl.ds(pl.multiple_of(t * CHUNK * feat, CHUNK * feat), CHUNK * feat)
        return acc[rows, :].reshape(CHUNK, feat, LANES)

    def begin(t, _):
        gathered = moment_at(t)[:, :, feat : feat + 1]
        vec[at(t), :] = jnp.sum(voxel[at(t)] * gathered, axis=1)
        return 0

    lax.fori_loop(0, chunks, begin, 0)

    masks = [adjacency_ref[:, k : k + 1] >= 0 for k in range(4)]
    degree = sum(jnp.where(m, 1.0, 0.0) for m in masks)
    here = [ix > 0, ix < gx - 1, iy > 0, iy < gy - 1]
    beside = [(ix - 1, iy), (ix + 1, iy), (ix, iy - 1), (ix, iy + 1)]

    def halo_copy(step, k):
        if k < 2:
            source = z_ref.at[step, pl.ds(k * (bricks - 8), 8)]
        else:
            source = y_send.at[step, k - 2]
        return pltpu.make_async_remote_copy(
            src_ref=source,
            dst_ref=halo.at[step, k ^ 1],
            send_sem=halo_send.at[step, k],
            recv_sem=halo_recv.at[step, k ^ 1],
            device_id=beside[k],
            device_id_type=MESH,
        )

    def halo_arrived(step, k):
        return pltpu.make_async_remote_copy(
            src_ref=y_send.at[step, 0],
            dst_ref=halo.at[step, k],
            send_sem=halo_send.at[step, k],
            recv_sem=halo_recv.at[step, k],
            device_id=beside[k],
            device_id_type=MESH,
        )

    def part_copy(step, to, frm):
        return pltpu.make_async_remote_copy(
            src_ref=part.at[step],
            dst_ref=parts.at[step, frm],
            send_sem=part_send.at[step, to],
            recv_sem=part_recv.at[step, frm],
            device_id=place(to),
            device_id_type=MESH,
        )

    def operate(step):
        def project(t, _):
            column = jnp.sum(voxel[at(t)] * vec[at(t), :][:, None, :], axis=2, keepdims=True)
            z_ref[step, at(t), :] = jnp.sum(jnp.where(eye, column, 0.0), axis=1)
            my_ref[at(t), :] = jnp.sum(moment_at(t) * column, axis=1)
            return 0

        lax.fori_loop(0, chunks, project, 0)
        for e in range(2):
            y_send[step, e] = z_ref[step, pl.ds(e * (BY - 1), BX, stride=BY), :]
        for k in range(4):

            @pl.when(here[k])
            def _():
                halo_copy(step, k).start()

        z = z_ref[step]
        ym_ref[1:bricks, :] = z[: bricks - 1]
        yp_ref[0 : bricks - 1, :] = z[1:]
        for k in range(4):

            @pl.when(here[k])
            def _():
                halo_arrived(step, k).wait_recv()

        xm = jnp.concatenate([halo[step, 0][8 - BY :], z[: bricks - BY]], axis=0)
        xp = jnp.concatenate([z[BY:], halo[step, 1][:BY]], axis=0)
        ym_ref[pl.ds(0, BX, stride=BY), :] = halo[step, 2]
        yp_ref[pl.ds(BY - 1, BX, stride=BY), :] = halo[step, 3]
        near = jnp.where(masks[0], xm, 0.0) + jnp.where(masks[1], xp, 0.0)
        near = near + jnp.where(masks[2], ym_ref[...], 0.0) + jnp.where(masks[3], yp_ref[...], 0.0)
        mid_ref[...] = my_ref[...] + coupling_weight * (degree * z - near)

        def expand(t, _):
            column = jnp.sum(
                jnp.where(eye, mid_ref[at(t), :][:, None, :], 0.0), axis=2, keepdims=True
            )
            back = jnp.sum(voxel[at(t)] * column, axis=1)
            image[at(t), :] = back + reg_ref[at(t), :] * vec[at(t), :]
            return 0

        lax.fori_loop(0, chunks, expand, 0)

    def fold(values):
        total = jnp.sum(values, axis=0, keepdims=True)
        width = total.shape[1]
        return sum(total[:, c : c + LANES] for c in range(0, width, LANES))

    def two_products(step):
        r, w = vec[...], image[...]
        mine = jnp.concatenate([fold(r * r), fold(r * w)], axis=0)
        part[step] = mine
        parts[step, me] = mine

        def start(j, _):
            part_copy(step, (me + j) % count, me).start()
            return 0

        lax.fori_loop(1, count, start, 0)

        def finish(j, _):
            source = (me + count - j) % count
            part_copy(step, source, source).wait_recv()
            return 0

        lax.fori_loop(1, count, finish, 0)
        total = jnp.sum(jnp.sum(parts[step], axis=0), axis=1, keepdims=True)
        return total[0:1], total[1:2]

    norm_now = alpha = None
    for step in range(ITERS):
        operate(step)
        norm, product = two_products(step)
        if step == 0:
            alpha = norm / product
            d, c = vec[...], image[...]
            solution_ref[...] = alpha * d
        else:
            ratio = norm / norm_now
            alpha = norm / (product - ratio * norm / alpha)
            d = vec[...] + ratio * direction[...]
            c = image[...] + ratio * carried[...]
            solution_ref[...] += alpha * d
        r = vec[...] - alpha * c
        if step + 1 < ITERS:
            vec[...] = r
            direction[...] = d
            carried[...] = c
        else:
            residual_ref[...] = r
        norm_now = norm

    def drain(j, _):
        to = (me + j) % count
        feat_copy(to, me).wait_send()
        extra_copy(to, me).wait_send()
        for step in range(ITERS):
            part_copy(step, to, me).wait_send()
        return 0

    lax.fori_loop(1, count, drain, 0)
    for step in range(ITERS):
        for k in range(4):

            @pl.when(here[k])
            def _():
                halo_copy(step, k).wait_send()


def shards(gx, gy, point_feats, point_targets, point_lists, brick_adjacency, voxel_feats, voxel_reg):
    feat = point_feats.shape[0]
    brick_total, slots = point_lists.shape
    bricks, _, vox = voxel_feats.shape
    count = gx * gy
    cols = bricks * slots
    offset = point_lists - jnp.arange(brick_total, dtype=jnp.int32)[:, None] * slots
    offset = jnp.where(point_lists >= 0, offset, -1)
    live = jnp.any(
        offset[:, :, None] == jnp.arange(slots, dtype=jnp.int32)[None, None, :], axis=1
    ).astype(jnp.bfloat16)
    extra = jnp.stack([live.reshape(count, cols), point_targets.reshape(count, cols)], axis=1)
    vmem = pl.BlockSpec(memory_space=pltpu.VMEM)
    hbm = pl.BlockSpec(memory_space=pl.ANY)
    f32 = jnp.float32
    return pl.pallas_call(
        functools.partial(kernel, gx, gy),
        out_shape=(jax.ShapeDtypeStruct((bricks, vox), f32),) * 2,
        in_specs=[hbm, hbm, vmem, hbm, vmem],
        out_specs=(vmem, vmem),
        scratch_shapes=[
            pltpu.VMEM((count, feat, cols), jnp.bfloat16),
            pltpu.VMEM((count, 2, cols), jnp.bfloat16),
            pltpu.VMEM((bricks, feat, vox), f32),
            pltpu.VMEM((bricks * feat, LANES), f32),
            pltpu.VMEM((bricks, vox), f32),
            pltpu.VMEM((bricks, vox), f32),
            pltpu.VMEM((bricks, vox), f32),
            pltpu.VMEM((bricks, vox), f32),
            pltpu.VMEM((ITERS, bricks, LANES), f32),
            pltpu.VMEM((bricks, LANES), f32),
            pltpu.VMEM((bricks, LANES), f32),
            pltpu.VMEM((bricks, LANES), f32),
            pltpu.VMEM((bricks, LANES), f32),
            pltpu.VMEM((ITERS, 2, BX, LANES), f32),
            pltpu.VMEM((ITERS, 4, 8, LANES), f32),
            pltpu.VMEM((ITERS, 2, LANES), f32),
            pltpu.VMEM((ITERS, count, 2, LANES), f32),
            pltpu.SemaphoreType.DMA,
            pltpu.SemaphoreType.DMA((count,)),
            pltpu.SemaphoreType.DMA((count,)),
            pltpu.SemaphoreType.DMA((count,)),
            pltpu.SemaphoreType.DMA((count,)),
            pltpu.SemaphoreType.DMA((ITERS, 4)),
            pltpu.SemaphoreType.DMA((ITERS, 4)),
            pltpu.SemaphoreType.DMA((ITERS, count)),
            pltpu.SemaphoreType.DMA((ITERS, count)),
        ],
        compiler_params=pltpu.CompilerParams(collective_id=0, has_side_effects=True),
    )(point_feats, extra, brick_adjacency, voxel_feats, voxel_reg)


def solution(mesh):
    placed = (
        P(None, ("gx", "gy")),
        P(("gx", "gy")),
        P(("gx", "gy"), None),
        P(("gx", "gy"), None),
        P(("gx", "gy"), None, None),
        P(("gx", "gy"), None),
    )
    return jax.shard_map(
        functools.partial(shards, mesh.shape["gx"], mesh.shape["gy"]),
        mesh=mesh,
        in_specs=placed,
        out_specs=(P(("gx", "gy"), None), P(("gx", "gy"), None)),
        check_vma=False,
    )
```

```python
import functools
import math

import jax
import jax.numpy as jnp
from jax import lax
from jax.experimental import pallas as pl
from jax.experimental.pallas import tpu as pltpu
from jax.sharding import PartitionSpec as P

BX = 8
BY = 4
ITERS = 3
LANES = 128
CHUNK = 8
MESH = pl.DeviceIdType.MESH
STRIDE = 1
SCALE = 2.0**-8
SHIFTS = (8.0, 1.0, 4.0)

coupling_weight = 1.0


def kernel(
    gx,
    gy,
    feats_hbm,
    target_ref,
    lists_ref,
    adjacency_ref,
    voxel_hbm,
    reg_ref,
    solution_ref,
    residual_ref,
    got,
    got_extra,
    extra,
    flat,
    voxel,
    acc,
    basis,
    z_ref,
    my_ref,
    mid_ref,
    ym_ref,
    yp_ref,
    y_send,
    halo,
    part,
    parts,
    voxel_sem,
    feat_send,
    feat_recv,
    extra_send,
    extra_recv,
    halo_send,
    halo_recv,
    part_send,
    part_recv,
):
    count = gx * gy
    ix, iy = lax.axis_index("gx"), lax.axis_index("gy")
    me = ix * gy + iy
    feat, cols = got.shape[1], got.shape[2]
    bricks = reg_ref.shape[0]
    slots = cols // bricks
    halves = cols // LANES
    per_half = LANES // slots

    step_by = STRIDE if math.gcd(STRIDE, count) == 1 else 1

    def place(index):
        return (index // gy, index % gy)

    barrier = pltpu.get_barrier_semaphore()

    def greet(j, _):
        pl.semaphore_signal(
            barrier, inc=1, device_id=place((me + j * step_by) % count), device_id_type=MESH
        )
        return 0

    lax.fori_loop(1, count, greet, 0)
    voxel_copy = pltpu.make_async_copy(voxel_hbm, voxel, voxel_sem)
    voxel_copy.start()
    halo[...] = jnp.zeros_like(halo)
    acc[...] = jnp.zeros_like(acc)
    own_feat = pltpu.make_async_copy(
        feats_hbm.at[:, pl.ds(pl.multiple_of(me * cols, cols), cols)], got.at[me], feat_recv.at[me]
    )
    own_extra = pltpu.make_async_copy(extra.at[me], got_extra.at[me], extra_recv.at[me])
    own_feat.start()

    total_bricks = lists_ref.shape[1]
    groups = total_bricks // LANES
    wide = slots * LANES
    listed = lists_ref[...]
    offset = listed - slots * lax.broadcasted_iota(jnp.int32, listed.shape, 1)
    offset = jnp.where(listed >= 0, offset, -1)
    hits = jnp.concatenate(
        [
            jnp.max(jnp.where(offset == d, 1.0, 0.0), axis=0, keepdims=True)
            for d in range(slots)
        ],
        axis=0,
    )
    hits = jnp.concatenate(
        [hits[:, g * LANES : (g + 1) * LANES] for g in range(groups)], axis=0
    ).astype(jnp.bfloat16)
    spread = jnp.where(
        lax.broadcasted_iota(jnp.int32, (LANES, wide), 1) // slots
        == lax.broadcasted_iota(jnp.int32, (LANES, wide), 0),
        1.0,
        0.0,
    ).astype(jnp.bfloat16)
    spread_hits = jnp.dot(hits, spread, preferred_element_type=jnp.float32)
    same = (
        lax.broadcasted_iota(jnp.int32, (slots, wide), 1) % slots
        == lax.broadcasted_iota(jnp.int32, (slots, wide), 0)
    )
    live_rows = jnp.sum(
        jnp.where(same[None], spread_hits.reshape(groups, slots, wide), 0.0), axis=1
    )
    for l in range(slots):
        flat[pl.ds(l, groups, stride=slots), :] = live_rows[:, l * LANES : (l + 1) * LANES]
    targets = target_ref[...].astype(jnp.float32)
    for k in range(count):
        rows = slice(k * halves, (k + 1) * halves)
        extra[k] = jnp.concatenate([flat[rows, :], targets[rows]], axis=0).astype(jnp.bfloat16)
    own_extra.start()
    pl.semaphore_wait(barrier, count - 1)

    def feat_copy(to, frm):
        return pltpu.make_async_remote_copy(
            src_ref=feats_hbm.at[:, pl.ds(pl.multiple_of(to * cols, cols), cols)],
            dst_ref=got.at[frm],
            send_sem=feat_send.at[to],
            recv_sem=feat_recv.at[frm],
            device_id=place(to),
            device_id_type=MESH,
        )

    def extra_copy(to, frm):
        return pltpu.make_async_remote_copy(
            src_ref=extra.at[to],
            dst_ref=got_extra.at[frm],
            send_sem=extra_send.at[to],
            recv_sem=extra_recv.at[frm],
            device_id=place(to),
            device_id_type=MESH,
        )

    def send(j, _):
        to = (me + j * step_by) % count
        feat_copy(to, me).start()
        extra_copy(to, me).start()
        return 0

    lax.fori_loop(1, count, send, 0)
    own_feat.wait()
    own_extra.wait()

    group = 4
    while count % group:
        group //= 2
    lane = lax.broadcasted_iota(jnp.int32, (1, group * LANES), 1)
    owner = (lane // slots) % per_half

    def absorb(g, _):
        sources = []
        for u in range(group):
            j = g * group + u
            source = (me + (count - j) * step_by) % count
            sources.append(source)
            if u:
                feat_copy(source, source).wait_recv()
                extra_copy(source, source).wait_recv()
            else:

                @pl.when(g > 0)
                def _():
                    feat_copy(source, source).wait_recv()
                    extra_copy(source, source).wait_recv()

        for h in range(halves):
            span = slice(h * LANES, (h + 1) * LANES)
            x = jnp.concatenate([got[s, :, span] for s in sources], axis=1)
            more = jnp.concatenate(
                [got_extra[s].astype(jnp.float32) for s in sources], axis=1
            )
            live = more[h : h + 1]
            target = more[halves + h : halves + h + 1].astype(jnp.bfloat16)
            left = jnp.concatenate(
                [x * jnp.where(owner == b, live, 0.0).astype(jnp.bfloat16) for b in range(per_half)],
                axis=0,
            )
            right = jnp.concatenate(
                [
                    x,
                    jnp.broadcast_to(target, (16, group * LANES)),
                    jnp.zeros((LANES - feat - 16, group * LANES), jnp.bfloat16),
                ],
                axis=0,
            )
            rows = slice(h * per_half * feat, (h + 1) * per_half * feat)
            acc[rows, :] += lax.dot_general(
                left, right, (((1,), (1,)), ((), ())), preferred_element_type=jnp.float32
            )
        return 0

    lax.fori_loop(0, count // group, absorb, 0)
    voxel_copy.wait()

    eye = lax.broadcasted_iota(jnp.int32, (1, feat, LANES), 1) == lax.broadcasted_iota(
        jnp.int32, (1, feat, LANES), 2
    )
    chunks = bricks // CHUNK

    def at(t):
        return pl.ds(pl.multiple_of(t * CHUNK, CHUNK), CHUNK)

    def moment_at(t):
        rows = pl.ds(pl.multiple_of(t * CHUNK * feat, CHUNK * feat), CHUNK * feat)
        return acc[rows, :].reshape(CHUNK, feat, LANES)

    def begin(t, _):
        gathered = moment_at(t)[:, :, feat : feat + 1]
        basis[0, at(t), :] = jnp.sum(voxel[at(t)] * gathered, axis=1)
        return 0

    lax.fori_loop(0, chunks, begin, 0)

    linked = jnp.where(adjacency_ref[...] >= 0, 1.0, 0.0)
    same_brick = lax.broadcasted_iota(jnp.int32, (bricks, bricks), 0) == lax.broadcasted_iota(
        jnp.int32, (bricks, bricks), 1
    )
    weights = [
        jnp.sum(jnp.where(same_brick, linked[k : k + 1], 0.0), axis=1, keepdims=True)
        for k in range(4)
    ]
    masks = [w > 0.0 for w in weights]
    degree = weights[0] + weights[1] + weights[2] + weights[3]
    here = [ix > 0, ix < gx - 1, iy > 0, iy < gy - 1]
    beside = [(ix - 1, iy), (ix + 1, iy), (ix, iy - 1), (ix, iy + 1)]

    def halo_copy(step, k):
        if k < 2:
            source = z_ref.at[step, pl.ds(k * (bricks - 8), 8)]
        else:
            source = y_send.at[step, k - 2]
        return pltpu.make_async_remote_copy(
            src_ref=source,
            dst_ref=halo.at[step, k ^ 1],
            send_sem=halo_send.at[step, k],
            recv_sem=halo_recv.at[step, k ^ 1],
            device_id=beside[k],
            device_id_type=MESH,
        )

    def halo_arrived(step, k):
        return pltpu.make_async_remote_copy(
            src_ref=y_send.at[step, 0],
            dst_ref=halo.at[step, k],
            send_sem=halo_send.at[step, k],
            recv_sem=halo_recv.at[step, k],
            device_id=beside[k],
            device_id_type=MESH,
        )

    def part_copy(to, frm):
        return pltpu.make_async_remote_copy(
            src_ref=part,
            dst_ref=parts.at[frm],
            send_sem=part_send.at[to],
            recv_sem=part_recv.at[frm],
            device_id=place(to),
            device_id_type=MESH,
        )

    def operate(step):
        def project(t, _):
            column = jnp.sum(voxel[at(t)] * basis[step, at(t), :][:, None, :], axis=2, keepdims=True)
            z_ref[step, at(t), :] = jnp.sum(jnp.where(eye, column, 0.0), axis=1)
            my_ref[at(t), :] = jnp.sum(moment_at(t) * column, axis=1)
            return 0

        lax.fori_loop(0, chunks, project, 0)
        for e in range(2):
            y_send[step, e] = z_ref[step, pl.ds(e * (BY - 1), BX, stride=BY), :]
        for k in range(4):

            @pl.when(here[k])
            def _():
                halo_copy(step, k).start()

        z = z_ref[step]
        ym_ref[1:bricks, :] = z[: bricks - 1]
        yp_ref[0 : bricks - 1, :] = z[1:]
        for k in range(4):

            @pl.when(here[k])
            def _():
                halo_arrived(step, k).wait_recv()

        xm = jnp.concatenate([halo[step, 0][8 - BY :], z[: bricks - BY]], axis=0)
        xp = jnp.concatenate([z[BY:], halo[step, 1][:BY]], axis=0)
        ym_ref[pl.ds(0, BX, stride=BY), :] = halo[step, 2]
        yp_ref[pl.ds(BY - 1, BX, stride=BY), :] = halo[step, 3]
        near = jnp.where(masks[0], xm, 0.0) + jnp.where(masks[1], xp, 0.0)
        near = near + jnp.where(masks[2], ym_ref[...], 0.0) + jnp.where(masks[3], yp_ref[...], 0.0)
        mid_ref[...] = my_ref[...] + coupling_weight * (degree * z - near)

        def expand(t, _):
            column = jnp.sum(
                jnp.where(eye, mid_ref[at(t), :][:, None, :], 0.0), axis=2, keepdims=True
            )
            back = jnp.sum(voxel[at(t)] * column, axis=1)
            shifted = (reg_ref[at(t), :] - SHIFTS[step]) * basis[step, at(t), :]
            basis[step + 1, at(t), :] = SCALE * (back + shifted)
            return 0

        lax.fori_loop(0, chunks, expand, 0)

    def fold(values):
        total = jnp.sum(values, axis=0, keepdims=True)
        width = total.shape[1]
        return sum(total[:, c : c + LANES] for c in range(0, width, LANES))

    for step in range(ITERS):
        operate(step)

    pairs = [(a, b) for a in range(ITERS) for b in range(a, ITERS + 1)]
    rows = [fold(basis[a] * basis[b]) for a, b in pairs]
    rows = rows + [jnp.zeros_like(rows[0])] * (-len(rows) % 8)
    sums = jnp.sum(jnp.concatenate(rows, axis=0), axis=1, keepdims=True)
    entry = lax.broadcasted_iota(jnp.int32, (len(rows), LANES), 1)
    diagonal = entry == lax.broadcasted_iota(jnp.int32, (len(rows), LANES), 0)
    mine = jnp.sum(jnp.where(diagonal, sums, 0.0), axis=0, keepdims=True)
    part[...] = mine
    parts[me] = mine

    def start(j, _):
        part_copy((me + j * step_by) % count, me).start()
        return 0

    lax.fori_loop(1, count, start, 0)

    def finish(j, _):
        source = (me + (count - j) * step_by) % count
        part_copy(source, source).wait_recv()
        return 0

    lax.fori_loop(1, count, finish, 0)
    total = jnp.sum(parts[...], axis=0)
    spread_total = jnp.sum(
        jnp.where(diagonal, jnp.broadcast_to(total, diagonal.shape), 0.0), axis=1, keepdims=True
    )
    gram = {}
    for e, (a, b) in enumerate(pairs):
        gram[a, b] = gram[b, a] = spread_total[e : e + 1]

    def inner(left, right):
        terms = [
            left[a] * right[b] * gram[a, b] for a in range(len(left)) for b in range(len(right))
        ]
        return functools.reduce(lambda p, q: p + q, terms)

    def apply(coefficients):
        size = len(coefficients)
        out = [SHIFTS[k] * coefficients[k] for k in range(size)]
        out.append(coefficients[-1] * (1.0 / SCALE))
        for k in range(1, size):
            out[k] = out[k] + coefficients[k - 1] * (1.0 / SCALE)
        return out

    one = jnp.ones((1, 1), jnp.float32)
    res, direction, answer = [one], [one], []
    norm_now = gram[0, 0]
    for step in range(ITERS):
        image = apply(direction)
        alpha = norm_now / inner(direction, image)
        padded = answer + [jnp.zeros_like(one)] * (len(direction) - len(answer))
        answer = [p + alpha * d for p, d in zip(padded, direction)]
        res = [p - alpha * w for p, w in zip(res + [jnp.zeros_like(one)], image)]
        if step + 1 < ITERS:
            norm_next = inner(res, res)
            ratio = norm_next / norm_now
            direction = [
                p + ratio * d for p, d in zip(res, direction + [jnp.zeros_like(one)])
            ]
            norm_now = norm_next
    solution_ref[...] = functools.reduce(
        lambda p, q: p + q, [c * basis[k] for k, c in enumerate(answer)]
    )
    residual_ref[...] = functools.reduce(
        lambda p, q: p + q, [c * basis[k] for k, c in enumerate(res)]
    )

    def drain(j, _):
        to = (me + j * step_by) % count
        feat_copy(to, me).wait_send()
        extra_copy(to, me).wait_send()
        part_copy(to, me).wait_send()
        return 0

    lax.fori_loop(1, count, drain, 0)
    for step in range(ITERS):
        for k in range(4):

            @pl.when(here[k])
            def _():
                halo_copy(step, k).wait_send()


def shards(gx, gy, point_feats, point_targets, point_lists, brick_adjacency, voxel_feats, voxel_reg):
    feat = point_feats.shape[0]
    brick_total, slots = point_lists.shape
    bricks, _, vox = voxel_feats.shape
    count = gx * gy
    cols = bricks * slots
    vmem = pl.BlockSpec(memory_space=pltpu.VMEM)
    hbm = pl.BlockSpec(memory_space=pl.ANY)
    f32 = jnp.float32
    return pl.pallas_call(
        functools.partial(kernel, gx, gy),
        out_shape=(jax.ShapeDtypeStruct((bricks, vox), f32),) * 2,
        in_specs=[hbm, vmem, vmem, vmem, hbm, vmem],
        out_specs=(vmem, vmem),
        scratch_shapes=[
            pltpu.VMEM((count, feat, cols), jnp.bfloat16),
            pltpu.VMEM((count, 2 * cols // LANES, LANES), jnp.bfloat16),
            pltpu.VMEM((count, 2 * cols // LANES, LANES), jnp.bfloat16),
            pltpu.VMEM((count * cols // LANES, LANES), f32),
            pltpu.VMEM((bricks, feat, vox), f32),
            pltpu.VMEM((bricks * feat, LANES), f32),
            pltpu.VMEM((ITERS + 1, bricks, vox), f32),
            pltpu.VMEM((ITERS, bricks, LANES), f32),
            pltpu.VMEM((bricks, LANES), f32),
            pltpu.VMEM((bricks, LANES), f32),
            pltpu.VMEM((bricks, LANES), f32),
            pltpu.VMEM((bricks, LANES), f32),
            pltpu.VMEM((ITERS, 2, BX, LANES), f32),
            pltpu.VMEM((ITERS, 4, 8, LANES), f32),
            pltpu.VMEM((1, LANES), f32),
            pltpu.VMEM((count, 1, LANES), f32),
            pltpu.SemaphoreType.DMA,
            pltpu.SemaphoreType.DMA((count,)),
            pltpu.SemaphoreType.DMA((count,)),
            pltpu.SemaphoreType.DMA((count,)),
            pltpu.SemaphoreType.DMA((count,)),
            pltpu.SemaphoreType.DMA((ITERS, 4)),
            pltpu.SemaphoreType.DMA((ITERS, 4)),
            pltpu.SemaphoreType.DMA((count,)),
            pltpu.SemaphoreType.DMA((count,)),
        ],
        compiler_params=pltpu.CompilerParams(collective_id=0, has_side_effects=True),
    )(
        point_feats,
        point_targets.reshape(-1, LANES),
        point_lists.T,
        brick_adjacency.T,
        voxel_feats,
        voxel_reg,
    )


def solution(mesh):
    placed = (
        P(None, ("gx", "gy")),
        P(("gx", "gy")),
        P(("gx", "gy"), None),
        P(("gx", "gy"), None),
        P(("gx", "gy"), None, None),
        P(("gx", "gy"), None),
    )
    return jax.shard_map(
        functools.partial(shards, mesh.shape["gx"], mesh.shape["gy"]),
        mesh=mesh,
        in_specs=placed,
        out_specs=(P(("gx", "gy"), None), P(("gx", "gy"), None)),
        check_vma=False,
    )
```

```python
import functools
import math

import jax
import jax.numpy as jnp
from jax import lax
from jax.experimental import pallas as pl
from jax.experimental.pallas import tpu as pltpu
from jax.sharding import PartitionSpec as P

BX = 8
BY = 4
ITERS = 3
LANES = 128
CHUNK = 8
MESH = pl.DeviceIdType.MESH
STRIDE = 11
SCALE = 2.0**-8
SHIFTS = (8.0, 1.0, 4.0)

coupling_weight = 1.0


def kernel(
    gx,
    gy,
    feats_hbm,
    target_ref,
    lists_ref,
    adjacency_ref,
    voxel_hbm,
    reg_ref,
    answer_ref,
    res_ref,
    direction_ref,
    image_ref,
    alpha_ref,
    got,
    got_extra,
    extra,
    flat,
    voxel,
    acc,
    square,
    basis,
    z_ref,
    q_ref,
    my_ref,
    mid_ref,
    ym_ref,
    yp_ref,
    y_send,
    halo,
    part,
    parts,
    voxel_sem,
    feat_send,
    feat_recv,
    extra_send,
    extra_recv,
    halo_send,
    halo_recv,
    part_send,
    part_recv,
):
    count = gx * gy
    ix, iy = lax.axis_index("gx"), lax.axis_index("gy")
    me = ix * gy + iy
    feat, cols = got.shape[1], got.shape[2]
    bricks = reg_ref.shape[0]
    slots = cols // bricks
    halves = cols // LANES
    per_half = LANES // slots

    step_by = STRIDE if math.gcd(STRIDE, count) == 1 else 1

    def place(index):
        return (index // gy, index % gy)

    barrier = pltpu.get_barrier_semaphore()

    def greet(j, _):
        pl.semaphore_signal(
            barrier, inc=1, device_id=place((me + j * step_by) % count), device_id_type=MESH
        )
        return 0

    lax.fori_loop(1, count, greet, 0)
    voxel_copy = pltpu.make_async_copy(voxel_hbm, voxel, voxel_sem)
    voxel_copy.start()
    halo[...] = jnp.zeros_like(halo)
    acc[...] = jnp.zeros_like(acc)
    own_feat = pltpu.make_async_copy(
        feats_hbm.at[:, pl.ds(pl.multiple_of(me * cols, cols), cols)], got.at[me], feat_recv.at[me]
    )
    own_extra = pltpu.make_async_copy(extra.at[me], got_extra.at[me], extra_recv.at[me])
    own_feat.start()

    total_bricks = lists_ref.shape[1]
    groups = total_bricks // LANES
    wide = slots * LANES
    listed = lists_ref[...]
    offset = listed - slots * lax.broadcasted_iota(jnp.int32, listed.shape, 1)
    offset = jnp.where(listed >= 0, offset, -1)
    hits = jnp.concatenate(
        [
            jnp.max(jnp.where(offset == d, 1.0, 0.0), axis=0, keepdims=True)
            for d in range(slots)
        ],
        axis=0,
    )
    hits = jnp.concatenate(
        [hits[:, g * LANES : (g + 1) * LANES] for g in range(groups)], axis=0
    ).astype(jnp.bfloat16)
    spread = jnp.where(
        lax.broadcasted_iota(jnp.int32, (LANES, wide), 1) // slots
        == lax.broadcasted_iota(jnp.int32, (LANES, wide), 0),
        1.0,
        0.0,
    ).astype(jnp.bfloat16)
    spread_hits = jnp.dot(hits, spread, preferred_element_type=jnp.float32)
    same = (
        lax.broadcasted_iota(jnp.int32, (slots, wide), 1) % slots
        == lax.broadcasted_iota(jnp.int32, (slots, wide), 0)
    )
    live_rows = jnp.sum(
        jnp.where(same[None], spread_hits.reshape(groups, slots, wide), 0.0), axis=1
    )
    for l in range(slots):
        flat[pl.ds(l, groups, stride=slots), :] = live_rows[:, l * LANES : (l + 1) * LANES]
    targets = target_ref[...].astype(jnp.float32)
    for k in range(count):
        rows = slice(k * halves, (k + 1) * halves)
        extra[k] = jnp.concatenate([flat[rows, :], targets[rows]], axis=0).astype(jnp.bfloat16)
    own_extra.start()
    pl.semaphore_wait(barrier, count - 1)

    def feat_copy(to, frm):
        return pltpu.make_async_remote_copy(
            src_ref=feats_hbm.at[:, pl.ds(pl.multiple_of(to * cols, cols), cols)],
            dst_ref=got.at[frm],
            send_sem=feat_send.at[to],
            recv_sem=feat_recv.at[frm],
            device_id=place(to),
            device_id_type=MESH,
        )

    def extra_copy(to, frm):
        return pltpu.make_async_remote_copy(
            src_ref=extra.at[to],
            dst_ref=got_extra.at[frm],
            send_sem=extra_send.at[to],
            recv_sem=extra_recv.at[frm],
            device_id=place(to),
            device_id_type=MESH,
        )

    def send(j, _):
        to = (me + j * step_by) % count
        feat_copy(to, me).start()
        extra_copy(to, me).start()
        return 0

    lax.fori_loop(1, count, send, 0)
    voxel_copy.wait()
    square[...] = jnp.zeros_like(square)

    def squares(t, _):
        for u in range(4):
            b = t * 4 + u
            rows = pl.ds(pl.multiple_of(b * feat, feat), feat)
            square[rows, 0:feat] = lax.dot_general(
                voxel[b],
                voxel[b],
                (((1,), (1,)), ((), ())),
                precision=lax.Precision.HIGHEST,
                preferred_element_type=jnp.float32,
            )
        return 0

    lax.fori_loop(0, bricks // 4, squares, 0)
    own_feat.wait()
    own_extra.wait()

    group = 4
    while count % group:
        group //= 2
    lane = lax.broadcasted_iota(jnp.int32, (1, group * LANES), 1)
    owner = (lane // slots) % per_half

    def absorb(g, _):
        sources = []
        for u in range(group):
            j = g * group + u
            source = (me + (count - j) * step_by) % count
            sources.append(source)
            if u:
                feat_copy(source, source).wait_recv()
                extra_copy(source, source).wait_recv()
            else:

                @pl.when(g > 0)
                def _():
                    feat_copy(source, source).wait_recv()
                    extra_copy(source, source).wait_recv()

        for h in range(halves):
            span = slice(h * LANES, (h + 1) * LANES)
            x = jnp.concatenate([got[s, :, span] for s in sources], axis=1)
            more = jnp.concatenate(
                [got_extra[s].astype(jnp.float32) for s in sources], axis=1
            )
            live = more[h : h + 1]
            target = more[halves + h : halves + h + 1].astype(jnp.bfloat16)
            left = jnp.concatenate(
                [x * jnp.where(owner == b, live, 0.0).astype(jnp.bfloat16) for b in range(per_half)],
                axis=0,
            )
            right = jnp.concatenate(
                [
                    x,
                    jnp.broadcast_to(target, (16, group * LANES)),
                    jnp.zeros((LANES - feat - 16, group * LANES), jnp.bfloat16),
                ],
                axis=0,
            )
            rows = slice(h * per_half * feat, (h + 1) * per_half * feat)
            acc[rows, :] += lax.dot_general(
                left, right, (((1,), (1,)), ((), ())), preferred_element_type=jnp.float32
            )
        return 0

    lax.fori_loop(0, count // group, absorb, 0)

    eye = lax.broadcasted_iota(jnp.int32, (1, feat, LANES), 1) == lax.broadcasted_iota(
        jnp.int32, (1, feat, LANES), 2
    )
    chunks = bricks // CHUNK

    def at(t):
        return pl.ds(pl.multiple_of(t * CHUNK, CHUNK), CHUNK)

    def block(ref, t):
        rows = pl.ds(pl.multiple_of(t * CHUNK * feat, CHUNK * feat), CHUNK * feat)
        return ref[rows, :].reshape(CHUNK, feat, LANES)

    def as_column(rows):
        return jnp.sum(jnp.where(eye, rows[:, None, :], 0.0), axis=2, keepdims=True)

    def gathered(t):
        return block(acc, t)[:, :, feat : feat + 1]

    def begin(t, _):
        z_ref[0, at(t), :] = jnp.sum(block(square, t) * gathered(t), axis=1)
        return 0

    lax.fori_loop(0, chunks, begin, 0)

    linked = jnp.where(adjacency_ref[...] >= 0, 1.0, 0.0)
    same_brick = lax.broadcasted_iota(jnp.int32, (bricks, bricks), 0) == lax.broadcasted_iota(
        jnp.int32, (bricks, bricks), 1
    )
    weights = [
        jnp.sum(jnp.where(same_brick, linked[k : k + 1], 0.0), axis=1, keepdims=True)
        for k in range(4)
    ]
    masks = [w > 0.0 for w in weights]
    degree = weights[0] + weights[1] + weights[2] + weights[3]
    here = [ix > 0, ix < gx - 1, iy > 0, iy < gy - 1]
    beside = [(ix - 1, iy), (ix + 1, iy), (ix, iy - 1), (ix, iy + 1)]

    def halo_copy(step, k):
        if k < 2:
            source = z_ref.at[step, pl.ds(k * (bricks - 8), 8)]
        else:
            source = y_send.at[step, k - 2]
        return pltpu.make_async_remote_copy(
            src_ref=source,
            dst_ref=halo.at[step, k ^ 1],
            send_sem=halo_send.at[step, k],
            recv_sem=halo_recv.at[step, k ^ 1],
            device_id=beside[k],
            device_id_type=MESH,
        )

    def halo_arrived(step, k):
        return pltpu.make_async_remote_copy(
            src_ref=y_send.at[step, 0],
            dst_ref=halo.at[step, k],
            send_sem=halo_send.at[step, k],
            recv_sem=halo_recv.at[step, k],
            device_id=beside[k],
            device_id_type=MESH,
        )

    def part_copy(to, frm):
        return pltpu.make_async_remote_copy(
            src_ref=part,
            dst_ref=parts.at[frm],
            send_sem=part_send.at[to],
            recv_sem=part_recv.at[frm],
            device_id=place(to),
            device_id_type=MESH,
        )

    def fold(values):
        total = jnp.sum(values, axis=0, keepdims=True)
        width = total.shape[1]
        return sum(total[:, c : c + LANES] for c in range(0, width, LANES))

    def next_basis(step, t):
        if step == 0:
            return jnp.sum(voxel[at(t)] * gathered(t), axis=1)
        back = jnp.sum(voxel[at(t)] * as_column(mid_ref[at(t), :]), axis=1)
        shifted = (reg_ref[at(t), :] - SHIFTS[step - 1]) * basis[step - 1, at(t), :]
        return SCALE * (back + shifted)

    def operate(step):
        for e in range(2):
            y_send[step, e] = z_ref[step, pl.ds(e * (BY - 1), BX, stride=BY), :]
        for k in range(4):

            @pl.when(here[k])
            def _():
                halo_copy(step, k).start()

        def widen(t, _):
            made = next_basis(step, t)
            basis[step, at(t), :] = made
            if step + 1 < ITERS:
                weighted = reg_ref[at(t), :] * made
                column = jnp.sum(voxel[at(t)] * weighted[:, None, :], axis=2, keepdims=True)
                q_ref[at(t), :] = jnp.sum(jnp.where(eye, column, 0.0), axis=1)
            my_ref[at(t), :] = jnp.sum(block(acc, t) * as_column(z_ref[step, at(t), :]), axis=1)
            return 0

        lax.fori_loop(0, chunks, widen, 0)
        z = z_ref[step]
        ym_ref[1:bricks, :] = z[: bricks - 1]
        yp_ref[0 : bricks - 1, :] = z[1:]
        found = []
        if step + 1 == ITERS:
            found = [fold(basis[a] * basis[b]) for a, b in early]
        for k in range(4):

            @pl.when(here[k])
            def _():
                halo_arrived(step, k).wait_recv()

        xm = jnp.concatenate([halo[step, 0][8 - BY :], z[: bricks - BY]], axis=0)
        xp = jnp.concatenate([z[BY:], halo[step, 1][:BY]], axis=0)
        ym_ref[pl.ds(0, BX, stride=BY), :] = halo[step, 2]
        yp_ref[pl.ds(BY - 1, BX, stride=BY), :] = halo[step, 3]
        near = jnp.where(masks[0], xm, 0.0) + jnp.where(masks[1], xp, 0.0)
        near = near + jnp.where(masks[2], ym_ref[...], 0.0) + jnp.where(masks[3], yp_ref[...], 0.0)
        mid_ref[...] = my_ref[...] + coupling_weight * (degree * z - near)

        if step + 1 < ITERS:

            def advance(t, _):
                back = jnp.sum(block(square, t) * as_column(mid_ref[at(t), :]), axis=1)
                shifted = q_ref[at(t), :] - SHIFTS[step] * z_ref[step, at(t), :]
                z_ref[step + 1, at(t), :] = SCALE * (back + shifted)
                return 0

            lax.fori_loop(0, chunks, advance, 0)
        else:

            def last(t, _):
                basis[step + 1, at(t), :] = next_basis(step + 1, t)
                return 0

            lax.fori_loop(0, chunks, last, 0)
        return found

    early = [(a, b) for a in range(ITERS) for b in range(a, ITERS)]
    late = [(a, ITERS) for a in range(ITERS)]
    pairs = early + late
    rows = []
    for step in range(ITERS):
        rows = operate(step)
    rows = rows + [fold(basis[a] * basis[b]) for a, b in late]
    rows = rows + [jnp.zeros_like(rows[0])] * (-len(rows) % 8)
    sums = jnp.sum(jnp.concatenate(rows, axis=0), axis=1, keepdims=True)
    entry = lax.broadcasted_iota(jnp.int32, (len(rows), LANES), 1)
    diagonal = entry == lax.broadcasted_iota(jnp.int32, (len(rows), LANES), 0)
    mine = jnp.sum(jnp.where(diagonal, sums, 0.0), axis=0, keepdims=True)
    part[...] = mine
    parts[me] = mine

    def start(j, _):
        part_copy((me + j * step_by) % count, me).start()
        return 0

    lax.fori_loop(1, count, start, 0)

    def finish(j, _):
        source = (me + (count - j) * step_by) % count
        part_copy(source, source).wait_recv()
        return 0

    lax.fori_loop(1, count, finish, 0)
    total = jnp.sum(parts[...], axis=0)
    spread_total = jnp.sum(
        jnp.where(diagonal, jnp.broadcast_to(total, diagonal.shape), 0.0), axis=1, keepdims=True
    )
    gram = {}
    for e, (a, b) in enumerate(pairs):
        gram[a, b] = gram[b, a] = spread_total[e : e + 1]

    def inner(left, right):
        terms = [
            left[a] * right[b] * gram[a, b] for a in range(len(left)) for b in range(len(right))
        ]
        return functools.reduce(lambda p, q: p + q, terms)

    def apply(coefficients):
        size = len(coefficients)
        out = [SHIFTS[k] * coefficients[k] for k in range(size)]
        out.append(coefficients[-1] * (1.0 / SCALE))
        for k in range(1, size):
            out[k] = out[k] + coefficients[k - 1] * (1.0 / SCALE)
        return out

    one = jnp.ones((1, 1), jnp.float32)
    res, direction, answer = [one], [one], []
    norm_now = gram[0, 0]
    for step in range(ITERS):
        before_answer, before_res = answer, res
        image = apply(direction)
        alpha = norm_now / inner(direction, image)
        padded = answer + [jnp.zeros_like(one)] * (len(direction) - len(answer))
        answer = [p + alpha * d for p, d in zip(padded, direction)]
        res = [p - alpha * w for p, w in zip(res + [jnp.zeros_like(one)], image)]
        if step + 1 < ITERS:
            norm_next = inner(res, res)
            ratio = norm_next / norm_now
            direction = [
                p + ratio * d for p, d in zip(res, direction + [jnp.zeros_like(one)])
            ]
            norm_now = norm_next
    def combine(coefficients):
        return functools.reduce(
            lambda p, q: p + q, [c * basis[k] for k, c in enumerate(coefficients)]
        )

    answer_ref[...] = combine(before_answer)
    res_ref[...] = combine(before_res)
    direction_ref[...] = combine(direction)
    image_ref[...] = combine(image)
    alpha_ref[...] = jnp.broadcast_to(alpha, alpha_ref.shape)

    def drain(j, _):
        to = (me + j * step_by) % count
        feat_copy(to, me).wait_send()
        extra_copy(to, me).wait_send()
        part_copy(to, me).wait_send()
        return 0

    lax.fori_loop(1, count, drain, 0)
    for step in range(ITERS):
        for k in range(4):

            @pl.when(here[k])
            def _():
                halo_copy(step, k).wait_send()


def shards(gx, gy, point_feats, point_targets, point_lists, brick_adjacency, voxel_feats, voxel_reg):
    feat = point_feats.shape[0]
    brick_total, slots = point_lists.shape
    bricks, _, vox = voxel_feats.shape
    count = gx * gy
    cols = bricks * slots
    vmem = pl.BlockSpec(memory_space=pltpu.VMEM)
    hbm = pl.BlockSpec(memory_space=pl.ANY)
    f32 = jnp.float32
    answer, res, direction, image, alpha = pl.pallas_call(
        functools.partial(kernel, gx, gy),
        out_shape=(jax.ShapeDtypeStruct((bricks, vox), f32),) * 4
        + (jax.ShapeDtypeStruct((1, vox), f32),),
        in_specs=[hbm, vmem, vmem, vmem, hbm, vmem],
        out_specs=(vmem,) * 5,
        scratch_shapes=[
            pltpu.VMEM((count, feat, cols), jnp.bfloat16),
            pltpu.VMEM((count, 2 * cols // LANES, LANES), jnp.bfloat16),
            pltpu.VMEM((count, 2 * cols // LANES, LANES), jnp.bfloat16),
            pltpu.VMEM((count * cols // LANES, LANES), f32),
            pltpu.VMEM((bricks, feat, vox), f32),
            pltpu.VMEM((bricks * feat, LANES), f32),
            pltpu.VMEM((bricks * feat, LANES), f32),
            pltpu.VMEM((ITERS + 1, bricks, vox), f32),
            pltpu.VMEM((ITERS, bricks, LANES), f32),
            pltpu.VMEM((bricks, LANES), f32),
            pltpu.VMEM((bricks, LANES), f32),
            pltpu.VMEM((bricks, LANES), f32),
            pltpu.VMEM((bricks, LANES), f32),
            pltpu.VMEM((bricks, LANES), f32),
            pltpu.VMEM((ITERS, 2, BX, LANES), f32),
            pltpu.VMEM((ITERS, 4, 8, LANES), f32),
            pltpu.VMEM((1, LANES), f32),
            pltpu.VMEM((count, 1, LANES), f32),
            pltpu.SemaphoreType.DMA,
            pltpu.SemaphoreType.DMA((count,)),
            pltpu.SemaphoreType.DMA((count,)),
            pltpu.SemaphoreType.DMA((count,)),
            pltpu.SemaphoreType.DMA((count,)),
            pltpu.SemaphoreType.DMA((ITERS, 4)),
            pltpu.SemaphoreType.DMA((ITERS, 4)),
            pltpu.SemaphoreType.DMA((count,)),
            pltpu.SemaphoreType.DMA((count,)),
        ],
        compiler_params=pltpu.CompilerParams(collective_id=0, has_side_effects=True),
    )(
        point_feats,
        point_targets.reshape(-1, LANES),
        point_lists.T,
        brick_adjacency.T,
        voxel_feats,
        voxel_reg,
    )
    return answer + alpha * direction, res - alpha * image


def solution(mesh):
    placed = (
        P(None, ("gx", "gy")),
        P(("gx", "gy")),
        P(("gx", "gy"), None),
        P(("gx", "gy"), None),
        P(("gx", "gy"), None, None),
        P(("gx", "gy"), None),
    )
    return jax.shard_map(
        functools.partial(shards, mesh.shape["gx"], mesh.shape["gy"]),
        mesh=mesh,
        in_specs=placed,
        out_specs=(P(("gx", "gy"), None), P(("gx", "gy"), None)),
        check_vma=False,
    )
```

```python
import functools
import math

import jax
import jax.numpy as jnp
from jax import lax
from jax.experimental import pallas as pl
from jax.experimental.pallas import tpu as pltpu
from jax.sharding import PartitionSpec as P

BX = 8
BY = 4
ITERS = 3
LANES = 128
CHUNK = 8
MESH = pl.DeviceIdType.MESH
STRIDE = 11
SCALE = 2.0**-8
SHIFTS = (8.0, 1.0, 4.0)

coupling_weight = 1.0


def kernel(
    gx,
    gy,
    feats_hbm,
    target_ref,
    lists_ref,
    adjacency_ref,
    voxel_hbm,
    reg_ref,
    answer_ref,
    res_ref,
    direction_ref,
    image_ref,
    alpha_ref,
    got,
    got_extra,
    extra,
    flat,
    voxel,
    acc,
    square,
    basis,
    z_ref,
    q_ref,
    my_ref,
    mid_ref,
    ym_ref,
    yp_ref,
    y_send,
    halo,
    part,
    parts,
    voxel_sem,
    feat_send,
    feat_recv,
    extra_send,
    extra_recv,
    halo_send,
    halo_recv,
    part_send,
    part_recv,
):
    count = gx * gy
    ix, iy = lax.axis_index("gx"), lax.axis_index("gy")
    me = ix * gy + iy
    feat, cols = got.shape[1], got.shape[2]
    bricks = reg_ref.shape[0]
    slots = cols // bricks
    halves = cols // LANES
    per_half = LANES // slots

    step_by = STRIDE if math.gcd(STRIDE, count) == 1 else 1

    def place(index):
        return (index // gy, index % gy)

    barrier = pltpu.get_barrier_semaphore()

    def greet(j, _):
        pl.semaphore_signal(
            barrier, inc=1, device_id=place((me + j * step_by) % count), device_id_type=MESH
        )
        return 0

    lax.fori_loop(1, count, greet, 0)
    voxel_copy = pltpu.make_async_copy(voxel_hbm, voxel, voxel_sem)
    voxel_copy.start()
    halo[...] = jnp.zeros_like(halo)
    acc[...] = jnp.zeros_like(acc)
    own_feat = pltpu.make_async_copy(
        feats_hbm.at[:, pl.ds(pl.multiple_of(me * cols, cols), cols)], got.at[me], feat_recv.at[me]
    )
    own_extra = pltpu.make_async_copy(extra.at[me], got_extra.at[me], extra_recv.at[me])
    own_feat.start()

    total_bricks = lists_ref.shape[1]
    groups = total_bricks // LANES
    wide = slots * LANES
    listed = lists_ref[...]
    offset = listed - slots * lax.broadcasted_iota(jnp.int32, listed.shape, 1)
    offset = jnp.where(listed >= 0, offset, -1)
    hits = jnp.concatenate(
        [
            jnp.max(jnp.where(offset == d, 1.0, 0.0), axis=0, keepdims=True)
            for d in range(slots)
        ],
        axis=0,
    )
    hits = jnp.concatenate(
        [hits[:, g * LANES : (g + 1) * LANES] for g in range(groups)], axis=0
    ).astype(jnp.bfloat16)
    spread = jnp.where(
        lax.broadcasted_iota(jnp.int32, (LANES, wide), 1) // slots
        == lax.broadcasted_iota(jnp.int32, (LANES, wide), 0),
        1.0,
        0.0,
    ).astype(jnp.bfloat16)
    spread_hits = jnp.dot(hits, spread, preferred_element_type=jnp.float32)
    same = (
        lax.broadcasted_iota(jnp.int32, (slots, wide), 1) % slots
        == lax.broadcasted_iota(jnp.int32, (slots, wide), 0)
    )
    live_rows = jnp.sum(
        jnp.where(same[None], spread_hits.reshape(groups, slots, wide), 0.0), axis=1
    )
    for l in range(slots):
        flat[pl.ds(l, groups, stride=slots), :] = live_rows[:, l * LANES : (l + 1) * LANES]
    targets = target_ref[...].astype(jnp.float32)
    for k in range(count):
        rows = slice(k * halves, (k + 1) * halves)
        extra[k] = jnp.concatenate([flat[rows, :], targets[rows]], axis=0).astype(jnp.bfloat16)
    own_extra.start()
    pl.semaphore_wait(barrier, count - 1)

    def feat_copy(to, frm):
        return pltpu.make_async_remote_copy(
            src_ref=feats_hbm.at[:, pl.ds(pl.multiple_of(to * cols, cols), cols)],
            dst_ref=got.at[frm],
            send_sem=feat_send.at[to],
            recv_sem=feat_recv.at[frm],
            device_id=place(to),
            device_id_type=MESH,
        )

    def extra_copy(to, frm):
        return pltpu.make_async_remote_copy(
            src_ref=extra.at[to],
            dst_ref=got_extra.at[frm],
            send_sem=extra_send.at[to],
            recv_sem=extra_recv.at[frm],
            device_id=place(to),
            device_id_type=MESH,
        )

    def send(j, _):
        to = (me + j * step_by) % count
        feat_copy(to, me).start()
        extra_copy(to, me).start()
        return 0

    lax.fori_loop(1, count, send, 0)
    voxel_copy.wait()
    square[...] = jnp.zeros_like(square)

    def squares(t, _):
        for u in range(4):
            b = t * 4 + u
            rows = pl.ds(pl.multiple_of(b * feat, feat), feat)
            square[rows, 0:feat] = lax.dot_general(
                voxel[b],
                voxel[b],
                (((1,), (1,)), ((), ())),
                precision=lax.Precision.HIGHEST,
                preferred_element_type=jnp.float32,
            )
        return 0

    lax.fori_loop(0, bricks // 4, squares, 0)
    own_feat.wait()
    own_extra.wait()

    group = 4
    while count % group:
        group //= 2
    lane = lax.broadcasted_iota(jnp.int32, (1, group * LANES), 1)
    owner = (lane // slots) % per_half

    def absorb(g, _):
        sources = []
        for u in range(group):
            j = g * group + u
            source = (me + (count - j) * step_by) % count
            sources.append(source)
            if u:
                feat_copy(source, source).wait_recv()
                extra_copy(source, source).wait_recv()
            else:

                @pl.when(g > 0)
                def _():
                    feat_copy(source, source).wait_recv()
                    extra_copy(source, source).wait_recv()

        for h in range(halves):
            span = slice(h * LANES, (h + 1) * LANES)
            x = jnp.concatenate([got[s, :, span] for s in sources], axis=1)
            more = jnp.concatenate(
                [got_extra[s].astype(jnp.float32) for s in sources], axis=1
            )
            live = more[h : h + 1]
            target = more[halves + h : halves + h + 1].astype(jnp.bfloat16)
            left = jnp.concatenate(
                [x * jnp.where(owner == b, live, 0.0).astype(jnp.bfloat16) for b in range(per_half)],
                axis=0,
            )
            right = jnp.concatenate(
                [
                    x,
                    jnp.broadcast_to(target, (16, group * LANES)),
                    jnp.zeros((LANES - feat - 16, group * LANES), jnp.bfloat16),
                ],
                axis=0,
            )
            rows = slice(h * per_half * feat, (h + 1) * per_half * feat)
            acc[rows, :] += lax.dot_general(
                left, right, (((1,), (1,)), ((), ())), preferred_element_type=jnp.float32
            )
        return 0

    lax.fori_loop(0, count // group, absorb, 0)

    eye = lax.broadcasted_iota(jnp.int32, (1, feat, LANES), 1) == lax.broadcasted_iota(
        jnp.int32, (1, feat, LANES), 2
    )
    chunks = bricks // CHUNK
    in_feat = lax.broadcasted_iota(jnp.int32, (bricks, LANES), 1) < feat

    def at(t):
        return pl.ds(pl.multiple_of(t * CHUNK, CHUNK), CHUNK)

    def block(ref, t):
        rows = pl.ds(pl.multiple_of(t * CHUNK * feat, CHUNK * feat), CHUNK * feat)
        return ref[rows, :].reshape(CHUNK, feat, LANES)

    def as_column(rows):
        return jnp.sum(jnp.where(eye, rows[:, None, :], 0.0), axis=2, keepdims=True)

    def gathered(t):
        return block(acc, t)[:, :, feat : feat + 1]

    def begin(t, _):
        z_ref[0, at(t), :] = jnp.sum(block(square, t) * gathered(t), axis=1)
        return 0

    lax.fori_loop(0, chunks, begin, 0, unroll=True)

    linked = jnp.where(adjacency_ref[...] >= 0, 1.0, 0.0)
    same_brick = lax.broadcasted_iota(jnp.int32, (bricks, bricks), 0) == lax.broadcasted_iota(
        jnp.int32, (bricks, bricks), 1
    )
    weights = [
        jnp.sum(jnp.where(same_brick, linked[k : k + 1], 0.0), axis=1, keepdims=True)
        for k in range(4)
    ]
    masks = [w > 0.0 for w in weights]
    degree = weights[0] + weights[1] + weights[2] + weights[3]
    here = [ix > 0, ix < gx - 1, iy > 0, iy < gy - 1]
    beside = [(ix - 1, iy), (ix + 1, iy), (ix, iy - 1), (ix, iy + 1)]

    def halo_copy(step, k):
        if k < 2:
            source = z_ref.at[step, pl.ds(k * (bricks - 8), 8)]
        else:
            source = y_send.at[step, k - 2]
        return pltpu.make_async_remote_copy(
            src_ref=source,
            dst_ref=halo.at[step, k ^ 1],
            send_sem=halo_send.at[step, k],
            recv_sem=halo_recv.at[step, k ^ 1],
            device_id=beside[k],
            device_id_type=MESH,
        )

    def halo_arrived(step, k):
        return pltpu.make_async_remote_copy(
            src_ref=y_send.at[step, 0],
            dst_ref=halo.at[step, k],
            send_sem=halo_send.at[step, k],
            recv_sem=halo_recv.at[step, k],
            device_id=beside[k],
            device_id_type=MESH,
        )

    def part_copy(to, frm):
        return pltpu.make_async_remote_copy(
            src_ref=part,
            dst_ref=parts.at[frm],
            send_sem=part_send.at[to],
            recv_sem=part_recv.at[frm],
            device_id=place(to),
            device_id_type=MESH,
        )

    def fold(values):
        total = jnp.sum(values, axis=0, keepdims=True)
        width = total.shape[1]
        return sum(total[:, c : c + LANES] for c in range(0, width, LANES))

    def next_basis(step, t):
        if step == 0:
            return jnp.sum(voxel[at(t)] * gathered(t), axis=1)
        back = jnp.sum(voxel[at(t)] * as_column(mid_ref[at(t), :]), axis=1)
        shifted = (reg_ref[at(t), :] - SHIFTS[step - 1]) * basis[step - 1, at(t), :]
        return SCALE * (back + shifted)

    def operate(step):
        for e in range(2):
            y_send[step, e] = z_ref[step, pl.ds(e * (BY - 1), BX, stride=BY), :]
        for k in range(4):

            @pl.when(here[k])
            def _():
                halo_copy(step, k).start()

        def widen(t, _):
            made = next_basis(step, t)
            basis[step, at(t), :] = made
            if step + 1 < ITERS:
                weighted = reg_ref[at(t), :] * made
                column = jnp.sum(voxel[at(t)] * weighted[:, None, :], axis=2, keepdims=True)
                q_ref[at(t), :] = jnp.sum(jnp.where(eye, column, 0.0), axis=1)
            my_ref[at(t), :] = jnp.sum(block(acc, t) * as_column(z_ref[step, at(t), :]), axis=1)
            return 0

        lax.fori_loop(0, chunks, widen, 0)
        z = z_ref[step]
        ym_ref[1:bricks, :] = z[: bricks - 1]
        yp_ref[0 : bricks - 1, :] = z[1:]
        found = []
        if step + 1 == ITERS:
            found = [fold(basis[a] * basis[b]) for a, b in early]
            final = (reg_ref[...] - SHIFTS[step]) * basis[step]
            found = found + [fold(basis[a] * final) for a, b in late]
        for k in range(4):

            @pl.when(here[k])
            def _():
                halo_arrived(step, k).wait_recv()

        xm = jnp.concatenate([halo[step, 0][8 - BY :], z[: bricks - BY]], axis=0)
        xp = jnp.concatenate([z[BY:], halo[step, 1][:BY]], axis=0)
        ym_ref[pl.ds(0, BX, stride=BY), :] = halo[step, 2]
        yp_ref[pl.ds(BY - 1, BX, stride=BY), :] = halo[step, 3]
        near = jnp.where(masks[0], xm, 0.0) + jnp.where(masks[1], xp, 0.0)
        near = near + jnp.where(masks[2], ym_ref[...], 0.0) + jnp.where(masks[3], yp_ref[...], 0.0)
        mid = jnp.where(in_feat, my_ref[...] + coupling_weight * (degree * z - near), 0.0)
        mid_ref[...] = mid

        if step + 1 < ITERS:

            def advance(t, _):
                back = jnp.sum(block(square, t) * as_column(mid_ref[at(t), :]), axis=1)
                shifted = q_ref[at(t), :] - SHIFTS[step] * z_ref[step, at(t), :]
                z_ref[step + 1, at(t), :] = SCALE * (back + shifted)
                return 0

            lax.fori_loop(0, chunks, advance, 0, unroll=True)
        else:
            for e, (a, b) in enumerate(late):
                e += len(early)
                found[e] = SCALE * (found[e] + fold(z_ref[a] * mid))
        return found

    early = [(a, b) for a in range(ITERS) for b in range(a, ITERS)]
    late = [(a, ITERS) for a in range(ITERS)]
    pairs = early + late
    rows = []
    for step in range(ITERS):
        rows = operate(step)
    rows = rows + [jnp.zeros_like(rows[0])] * (-len(rows) % 8)
    sums = jnp.sum(jnp.concatenate(rows, axis=0), axis=1, keepdims=True)
    entry = lax.broadcasted_iota(jnp.int32, (len(rows), LANES), 1)
    diagonal = entry == lax.broadcasted_iota(jnp.int32, (len(rows), LANES), 0)
    mine = jnp.sum(jnp.where(diagonal, sums, 0.0), axis=0, keepdims=True)
    part[...] = mine
    parts[me] = mine

    def start(j, _):
        part_copy((me + j * step_by) % count, me).start()
        return 0

    lax.fori_loop(1, count, start, 0)

    def last(t, _):
        basis[ITERS, at(t), :] = next_basis(ITERS, t)
        return 0

    lax.fori_loop(0, chunks, last, 0)

    def finish(j, _):
        source = (me + (count - j) * step_by) % count
        part_copy(source, source).wait_recv()
        return 0

    lax.fori_loop(1, count, finish, 0)
    total = jnp.sum(parts[...], axis=0)
    spread_total = jnp.sum(
        jnp.where(diagonal, jnp.broadcast_to(total, diagonal.shape), 0.0), axis=1, keepdims=True
    )
    gram = {}
    for e, (a, b) in enumerate(pairs):
        gram[a, b] = gram[b, a] = spread_total[e : e + 1]

    def inner(left, right):
        terms = [
            left[a] * right[b] * gram[a, b] for a in range(len(left)) for b in range(len(right))
        ]
        return functools.reduce(lambda p, q: p + q, terms)

    def apply(coefficients):
        size = len(coefficients)
        out = [SHIFTS[k] * coefficients[k] for k in range(size)]
        out.append(coefficients[-1] * (1.0 / SCALE))
        for k in range(1, size):
            out[k] = out[k] + coefficients[k - 1] * (1.0 / SCALE)
        return out

    one = jnp.ones((1, 1), jnp.float32)
    res, direction, answer = [one], [one], []
    norm_now = gram[0, 0]
    for step in range(ITERS):
        before_answer, before_res = answer, res
        image = apply(direction)
        alpha = norm_now / inner(direction, image)
        padded = answer + [jnp.zeros_like(one)] * (len(direction) - len(answer))
        answer = [p + alpha * d for p, d in zip(padded, direction)]
        res = [p - alpha * w for p, w in zip(res + [jnp.zeros_like(one)], image)]
        if step + 1 < ITERS:
            norm_next = inner(res, res)
            ratio = norm_next / norm_now
            direction = [
                p + ratio * d for p, d in zip(res, direction + [jnp.zeros_like(one)])
            ]
            norm_now = norm_next
    def combine(coefficients):
        return functools.reduce(
            lambda p, q: p + q, [c * basis[k] for k, c in enumerate(coefficients)]
        )

    answer_ref[...] = combine(before_answer)
    res_ref[...] = combine(before_res)
    direction_ref[...] = combine(direction)
    image_ref[...] = combine(image)
    alpha_ref[...] = jnp.broadcast_to(alpha, alpha_ref.shape)

    def drain(j, _):
        to = (me + j * step_by) % count
        feat_copy(to, me).wait_send()
        extra_copy(to, me).wait_send()
        part_copy(to, me).wait_send()
        return 0

    lax.fori_loop(1, count, drain, 0)
    for step in range(ITERS):
        for k in range(4):

            @pl.when(here[k])
            def _():
                halo_copy(step, k).wait_send()


def shards(gx, gy, point_feats, point_targets, point_lists, brick_adjacency, voxel_feats, voxel_reg):
    feat = point_feats.shape[0]
    brick_total, slots = point_lists.shape
    bricks, _, vox = voxel_feats.shape
    count = gx * gy
    cols = bricks * slots
    vmem = pl.BlockSpec(memory_space=pltpu.VMEM)
    hbm = pl.BlockSpec(memory_space=pl.ANY)
    f32 = jnp.float32
    answer, res, direction, image, alpha = pl.pallas_call(
        functools.partial(kernel, gx, gy),
        out_shape=(jax.ShapeDtypeStruct((bricks, vox), f32),) * 4
        + (jax.ShapeDtypeStruct((1, vox), f32),),
        in_specs=[hbm, vmem, vmem, vmem, hbm, vmem],
        out_specs=(vmem,) * 5,
        scratch_shapes=[
            pltpu.VMEM((count, feat, cols), jnp.bfloat16),
            pltpu.VMEM((count, 2 * cols // LANES, LANES), jnp.bfloat16),
            pltpu.VMEM((count, 2 * cols // LANES, LANES), jnp.bfloat16),
            pltpu.VMEM((count * cols // LANES, LANES), f32),
            pltpu.VMEM((bricks, feat, vox), f32),
            pltpu.VMEM((bricks * feat, LANES), f32),
            pltpu.VMEM((bricks * feat, LANES), f32),
            pltpu.VMEM((ITERS + 1, bricks, vox), f32),
            pltpu.VMEM((ITERS, bricks, LANES), f32),
            pltpu.VMEM((bricks, LANES), f32),
            pltpu.VMEM((bricks, LANES), f32),
            pltpu.VMEM((bricks, LANES), f32),
            pltpu.VMEM((bricks, LANES), f32),
            pltpu.VMEM((bricks, LANES), f32),
            pltpu.VMEM((ITERS, 2, BX, LANES), f32),
            pltpu.VMEM((ITERS, 4, 8, LANES), f32),
            pltpu.VMEM((1, LANES), f32),
            pltpu.VMEM((count, 1, LANES), f32),
            pltpu.SemaphoreType.DMA,
            pltpu.SemaphoreType.DMA((count,)),
            pltpu.SemaphoreType.DMA((count,)),
            pltpu.SemaphoreType.DMA((count,)),
            pltpu.SemaphoreType.DMA((count,)),
            pltpu.SemaphoreType.DMA((ITERS, 4)),
            pltpu.SemaphoreType.DMA((ITERS, 4)),
            pltpu.SemaphoreType.DMA((count,)),
            pltpu.SemaphoreType.DMA((count,)),
        ],
        compiler_params=pltpu.CompilerParams(collective_id=0, has_side_effects=True),
    )(
        point_feats,
        point_targets.reshape(-1, LANES),
        point_lists.T,
        brick_adjacency.T,
        voxel_feats,
        voxel_reg,
    )
    return answer + alpha * direction, res - alpha * image


def solution(mesh):
    placed = (
        P(None, ("gx", "gy")),
        P(("gx", "gy")),
        P(("gx", "gy"), None),
        P(("gx", "gy"), None),
        P(("gx", "gy"), None, None),
        P(("gx", "gy"), None),
    )
    return jax.shard_map(
        functools.partial(shards, mesh.shape["gx"], mesh.shape["gy"]),
        mesh=mesh,
        in_specs=placed,
        out_specs=(P(("gx", "gy"), None), P(("gx", "gy"), None)),
        check_vma=False,
    )
```

```python
import functools
import math

import jax
import jax.numpy as jnp
from jax import lax
from jax.experimental import pallas as pl
from jax.experimental.pallas import tpu as pltpu
from jax.sharding import PartitionSpec as P

BX = 8
BY = 4
ITERS = 3
LANES = 128
CHUNK = 8
MESH = pl.DeviceIdType.MESH
STRIDE = 11
SCALE = 2.0**-8
SHIFTS = (8.0, 1.0, 4.0)

coupling_weight = 1.0


def kernel(
    gx,
    gy,
    feats_hbm,
    target_ref,
    lists_ref,
    adjacency_ref,
    voxel_hbm,
    reg_ref,
    answer_ref,
    res_ref,
    direction_ref,
    image_ref,
    alpha_ref,
    got,
    got_extra,
    extra,
    flat,
    voxel,
    acc,
    square,
    basis,
    z_ref,
    q_ref,
    my_ref,
    mid_ref,
    ym_ref,
    yp_ref,
    y_send,
    halo,
    part,
    parts,
    voxel_sem,
    feat_send,
    feat_recv,
    extra_send,
    extra_recv,
    halo_send,
    halo_recv,
    part_send,
    part_recv,
):
    count = gx * gy
    ix, iy = lax.axis_index("gx"), lax.axis_index("gy")
    me = ix * gy + iy
    feat, cols = got.shape[1], got.shape[2]
    bricks = reg_ref.shape[0]
    slots = cols // bricks
    halves = cols // LANES
    per_half = LANES // slots

    step_by = STRIDE if math.gcd(STRIDE, count) == 1 else 1

    def place(index):
        return (index // gy, index % gy)

    barrier = pltpu.get_barrier_semaphore()

    def greet(j, _):
        pl.semaphore_signal(
            barrier, inc=1, device_id=place((me + j * step_by) % count), device_id_type=MESH
        )
        return 0

    lax.fori_loop(1, count, greet, 0, unroll=True)
    voxel_copy = pltpu.make_async_copy(voxel_hbm, voxel, voxel_sem)
    voxel_copy.start()
    halo[...] = jnp.zeros_like(halo)
    acc[...] = jnp.zeros_like(acc)
    own_feat = pltpu.make_async_copy(
        feats_hbm.at[:, pl.ds(pl.multiple_of(me * cols, cols), cols)], got.at[me], feat_recv.at[me]
    )
    own_extra = pltpu.make_async_copy(extra.at[me], got_extra.at[me], extra_recv.at[me])
    own_feat.start()

    total_bricks = lists_ref.shape[1]
    groups = total_bricks // LANES
    wide = slots * LANES
    listed = lists_ref[...]
    offset = listed - slots * lax.broadcasted_iota(jnp.int32, listed.shape, 1)
    offset = jnp.where(listed >= 0, offset, -1)
    hits = jnp.concatenate(
        [
            jnp.max(jnp.where(offset == d, 1.0, 0.0), axis=0, keepdims=True)
            for d in range(slots)
        ],
        axis=0,
    )
    hits = jnp.concatenate(
        [hits[:, g * LANES : (g + 1) * LANES] for g in range(groups)], axis=0
    ).astype(jnp.bfloat16)
    spread = jnp.where(
        lax.broadcasted_iota(jnp.int32, (LANES, wide), 1) // slots
        == lax.broadcasted_iota(jnp.int32, (LANES, wide), 0),
        1.0,
        0.0,
    ).astype(jnp.bfloat16)
    spread_hits = jnp.dot(hits, spread, preferred_element_type=jnp.float32)
    same = (
        lax.broadcasted_iota(jnp.int32, (slots, wide), 1) % slots
        == lax.broadcasted_iota(jnp.int32, (slots, wide), 0)
    )
    live_rows = jnp.sum(
        jnp.where(same[None], spread_hits.reshape(groups, slots, wide), 0.0), axis=1
    )
    for l in range(slots):
        flat[pl.ds(l, groups, stride=slots), :] = live_rows[:, l * LANES : (l + 1) * LANES]
    targets = target_ref[...].astype(jnp.float32)
    for k in range(count):
        rows = slice(k * halves, (k + 1) * halves)
        extra[k] = jnp.concatenate([flat[rows, :], targets[rows]], axis=0).astype(jnp.bfloat16)
    own_extra.start()
    pl.semaphore_wait(barrier, count - 1)

    def feat_copy(to, frm):
        return pltpu.make_async_remote_copy(
            src_ref=feats_hbm.at[:, pl.ds(pl.multiple_of(to * cols, cols), cols)],
            dst_ref=got.at[frm],
            send_sem=feat_send.at[to],
            recv_sem=feat_recv.at[frm],
            device_id=place(to),
            device_id_type=MESH,
        )

    def extra_copy(to, frm):
        return pltpu.make_async_remote_copy(
            src_ref=extra.at[to],
            dst_ref=got_extra.at[frm],
            send_sem=extra_send.at[to],
            recv_sem=extra_recv.at[frm],
            device_id=place(to),
            device_id_type=MESH,
        )

    def send(j, _):
        to = (me + j * step_by) % count
        feat_copy(to, me).start()
        extra_copy(to, me).start()
        return 0

    lax.fori_loop(1, count, send, 0)
    voxel_copy.wait()
    square[...] = jnp.zeros_like(square)

    def squares(t, _):
        for u in range(4):
            b = t * 4 + u
            rows = pl.ds(pl.multiple_of(b * feat, feat), feat)
            square[rows, 0:feat] = lax.dot_general(
                voxel[b],
                voxel[b],
                (((1,), (1,)), ((), ())),
                precision=lax.Precision.HIGHEST,
                preferred_element_type=jnp.float32,
            )
        return 0

    lax.fori_loop(0, bricks // 4, squares, 0)
    own_feat.wait()
    own_extra.wait()

    group = 4
    while count % group:
        group //= 2
    lane = lax.broadcasted_iota(jnp.int32, (1, group * LANES), 1)
    owner = (lane // slots) % per_half

    def absorb(g, _):
        sources = []
        for u in range(group):
            j = g * group + u
            source = (me + (count - j) * step_by) % count
            sources.append(source)
            if u:
                feat_copy(source, source).wait_recv()
                extra_copy(source, source).wait_recv()
            else:

                @pl.when(g > 0)
                def _():
                    feat_copy(source, source).wait_recv()
                    extra_copy(source, source).wait_recv()

        for h in range(halves):
            span = slice(h * LANES, (h + 1) * LANES)
            x = jnp.concatenate([got[s, :, span] for s in sources], axis=1)
            more = jnp.concatenate(
                [got_extra[s].astype(jnp.float32) for s in sources], axis=1
            )
            live = more[h : h + 1]
            target = more[halves + h : halves + h + 1].astype(jnp.bfloat16)
            left = jnp.concatenate(
                [x * jnp.where(owner == b, live, 0.0).astype(jnp.bfloat16) for b in range(per_half)],
                axis=0,
            )
            right = jnp.concatenate(
                [
                    x,
                    jnp.broadcast_to(target, (16, group * LANES)),
                    jnp.zeros((LANES - feat - 16, group * LANES), jnp.bfloat16),
                ],
                axis=0,
            )
            rows = slice(h * per_half * feat, (h + 1) * per_half * feat)
            acc[rows, :] += lax.dot_general(
                left, right, (((1,), (1,)), ((), ())), preferred_element_type=jnp.float32
            )
        return 0

    lax.fori_loop(0, count // group, absorb, 0)

    eye = lax.broadcasted_iota(jnp.int32, (1, feat, LANES), 1) == lax.broadcasted_iota(
        jnp.int32, (1, feat, LANES), 2
    )
    chunks = bricks // CHUNK
    in_feat = lax.broadcasted_iota(jnp.int32, (bricks, LANES), 1) < feat

    def at(t):
        return pl.ds(pl.multiple_of(t * CHUNK, CHUNK), CHUNK)

    def block(ref, t):
        rows = pl.ds(pl.multiple_of(t * CHUNK * feat, CHUNK * feat), CHUNK * feat)
        return ref[rows, :].reshape(CHUNK, feat, LANES)

    def as_column(rows):
        return jnp.sum(jnp.where(eye, rows[:, None, :], 0.0), axis=2, keepdims=True)

    def gathered(t):
        return block(acc, t)[:, :, feat : feat + 1]

    def begin(t, _):
        z_ref[0, at(t), :] = jnp.sum(block(square, t) * gathered(t), axis=1)
        return 0

    lax.fori_loop(0, chunks, begin, 0, unroll=True)

    linked = jnp.where(adjacency_ref[...] >= 0, 1.0, 0.0)
    same_brick = lax.broadcasted_iota(jnp.int32, (bricks, bricks), 0) == lax.broadcasted_iota(
        jnp.int32, (bricks, bricks), 1
    )
    weights = [
        jnp.sum(jnp.where(same_brick, linked[k : k + 1], 0.0), axis=1, keepdims=True)
        for k in range(4)
    ]
    masks = [w > 0.0 for w in weights]
    degree = weights[0] + weights[1] + weights[2] + weights[3]
    here = [ix > 0, ix < gx - 1, iy > 0, iy < gy - 1]
    beside = [(ix - 1, iy), (ix + 1, iy), (ix, iy - 1), (ix, iy + 1)]

    def halo_copy(step, k):
        if k < 2:
            source = z_ref.at[step, pl.ds(k * (bricks - 8), 8)]
        else:
            source = y_send.at[step, k - 2]
        return pltpu.make_async_remote_copy(
            src_ref=source,
            dst_ref=halo.at[step, k ^ 1],
            send_sem=halo_send.at[step, k],
            recv_sem=halo_recv.at[step, k ^ 1],
            device_id=beside[k],
            device_id_type=MESH,
        )

    def halo_arrived(step, k):
        return pltpu.make_async_remote_copy(
            src_ref=y_send.at[step, 0],
            dst_ref=halo.at[step, k],
            send_sem=halo_send.at[step, k],
            recv_sem=halo_recv.at[step, k],
            device_id=beside[k],
            device_id_type=MESH,
        )

    def part_copy(to, frm):
        return pltpu.make_async_remote_copy(
            src_ref=part,
            dst_ref=parts.at[frm],
            send_sem=part_send.at[to],
            recv_sem=part_recv.at[frm],
            device_id=place(to),
            device_id_type=MESH,
        )

    def fold(values):
        total = jnp.sum(values, axis=0, keepdims=True)
        width = total.shape[1]
        return sum(total[:, c : c + LANES] for c in range(0, width, LANES))

    def next_basis(step, t):
        if step == 0:
            return jnp.sum(voxel[at(t)] * gathered(t), axis=1)
        back = jnp.sum(voxel[at(t)] * as_column(mid_ref[at(t), :]), axis=1)
        shifted = (reg_ref[at(t), :] - SHIFTS[step - 1]) * basis[step - 1, at(t), :]
        return SCALE * (back + shifted)

    def operate(step):
        for e in range(2):
            y_send[step, e] = z_ref[step, pl.ds(e * (BY - 1), BX, stride=BY), :]
        for k in range(4):

            @pl.when(here[k])
            def _():
                halo_copy(step, k).start()

        def widen(t, _):
            made = next_basis(step, t)
            basis[step, at(t), :] = made
            if step + 1 < ITERS:
                weighted = reg_ref[at(t), :] * made
                column = jnp.sum(voxel[at(t)] * weighted[:, None, :], axis=2, keepdims=True)
                q_ref[at(t), :] = jnp.sum(jnp.where(eye, column, 0.0), axis=1)
            my_ref[at(t), :] = jnp.sum(block(acc, t) * as_column(z_ref[step, at(t), :]), axis=1)
            return 0

        lax.fori_loop(0, chunks, widen, 0)
        z = z_ref[step]
        ym_ref[1:bricks, :] = z[: bricks - 1]
        yp_ref[0 : bricks - 1, :] = z[1:]
        found = []
        if step + 1 == ITERS:
            found = [fold(basis[a] * basis[b]) for a, b in early]
            final = (reg_ref[...] - SHIFTS[step]) * basis[step]
            found = found + [fold(basis[a] * final) for a, b in late]
        for k in range(4):

            @pl.when(here[k])
            def _():
                halo_arrived(step, k).wait_recv()

        xm = jnp.concatenate([halo[step, 0][8 - BY :], z[: bricks - BY]], axis=0)
        xp = jnp.concatenate([z[BY:], halo[step, 1][:BY]], axis=0)
        ym_ref[pl.ds(0, BX, stride=BY), :] = halo[step, 2]
        yp_ref[pl.ds(BY - 1, BX, stride=BY), :] = halo[step, 3]
        near = jnp.where(masks[0], xm, 0.0) + jnp.where(masks[1], xp, 0.0)
        near = near + jnp.where(masks[2], ym_ref[...], 0.0) + jnp.where(masks[3], yp_ref[...], 0.0)
        mid = jnp.where(in_feat, my_ref[...] + coupling_weight * (degree * z - near), 0.0)
        mid_ref[...] = mid

        if step + 1 < ITERS:

            def advance(t, _):
                back = jnp.sum(block(square, t) * as_column(mid_ref[at(t), :]), axis=1)
                shifted = q_ref[at(t), :] - SHIFTS[step] * z_ref[step, at(t), :]
                z_ref[step + 1, at(t), :] = SCALE * (back + shifted)
                return 0

            lax.fori_loop(0, chunks, advance, 0, unroll=True)
        else:
            for e, (a, b) in enumerate(late):
                e += len(early)
                found[e] = SCALE * (found[e] + fold(z_ref[a] * mid))
        return found

    early = [(a, b) for a in range(ITERS) for b in range(a, ITERS)]
    late = [(a, ITERS) for a in range(ITERS)]
    pairs = early + late
    rows = []
    for step in range(ITERS):
        rows = operate(step)
    rows = rows + [jnp.zeros_like(rows[0])] * (-len(rows) % 8)
    sums = jnp.sum(jnp.concatenate(rows, axis=0), axis=1, keepdims=True)
    entry = lax.broadcasted_iota(jnp.int32, (len(rows), LANES), 1)
    diagonal = entry == lax.broadcasted_iota(jnp.int32, (len(rows), LANES), 0)
    mine = jnp.sum(jnp.where(diagonal, sums, 0.0), axis=0, keepdims=True)
    part[...] = mine
    parts[me] = mine

    def start(j, _):
        part_copy((me + j * step_by) % count, me).start()
        return 0

    lax.fori_loop(1, count, start, 0, unroll=True)

    def last(t, _):
        basis[ITERS, at(t), :] = next_basis(ITERS, t)
        return 0

    lax.fori_loop(0, chunks, last, 0)

    def finish(j, _):
        source = (me + (count - j) * step_by) % count
        part_copy(source, source).wait_recv()
        return 0

    lax.fori_loop(1, count, finish, 0)
    total = jnp.sum(parts[...], axis=0)
    spread_total = jnp.sum(
        jnp.where(diagonal, jnp.broadcast_to(total, diagonal.shape), 0.0), axis=1, keepdims=True
    )
    gram = {}
    for e, (a, b) in enumerate(pairs):
        gram[a, b] = gram[b, a] = spread_total[e : e + 1]

    def inner(left, right):
        terms = [
            left[a] * right[b] * gram[a, b] for a in range(len(left)) for b in range(len(right))
        ]
        return functools.reduce(lambda p, q: p + q, terms)

    def apply(coefficients):
        size = len(coefficients)
        out = [SHIFTS[k] * coefficients[k] for k in range(size)]
        out.append(coefficients[-1] * (1.0 / SCALE))
        for k in range(1, size):
            out[k] = out[k] + coefficients[k - 1] * (1.0 / SCALE)
        return out

    one = jnp.ones((1, 1), jnp.float32)
    res, direction, answer = [one], [one], []
    norm_now = gram[0, 0]
    for step in range(ITERS):
        before_answer, before_res = answer, res
        image = apply(direction)
        alpha = norm_now / inner(direction, image)
        padded = answer + [jnp.zeros_like(one)] * (len(direction) - len(answer))
        answer = [p + alpha * d for p, d in zip(padded, direction)]
        res = [p - alpha * w for p, w in zip(res + [jnp.zeros_like(one)], image)]
        if step + 1 < ITERS:
            norm_next = inner(res, res)
            ratio = norm_next / norm_now
            direction = [
                p + ratio * d for p, d in zip(res, direction + [jnp.zeros_like(one)])
            ]
            norm_now = norm_next
    def combine(coefficients):
        return functools.reduce(
            lambda p, q: p + q, [c * basis[k] for k, c in enumerate(coefficients)]
        )

    answer_ref[...] = combine(before_answer)
    res_ref[...] = combine(before_res)
    direction_ref[...] = combine(direction)
    image_ref[...] = combine(image)
    alpha_ref[...] = jnp.broadcast_to(alpha, alpha_ref.shape)

    def drain(j, _):
        to = (me + j * step_by) % count
        feat_copy(to, me).wait_send()
        extra_copy(to, me).wait_send()
        part_copy(to, me).wait_send()
        return 0

    lax.fori_loop(1, count, drain, 0)
    for step in range(ITERS):
        for k in range(4):

            @pl.when(here[k])
            def _():
                halo_copy(step, k).wait_send()


def shards(gx, gy, point_feats, point_targets, point_lists, brick_adjacency, voxel_feats, voxel_reg):
    feat = point_feats.shape[0]
    brick_total, slots = point_lists.shape
    bricks, _, vox = voxel_feats.shape
    count = gx * gy
    cols = bricks * slots
    vmem = pl.BlockSpec(memory_space=pltpu.VMEM)
    hbm = pl.BlockSpec(memory_space=pl.ANY)
    f32 = jnp.float32
    answer, res, direction, image, alpha = pl.pallas_call(
        functools.partial(kernel, gx, gy),
        out_shape=(jax.ShapeDtypeStruct((bricks, vox), f32),) * 4
        + (jax.ShapeDtypeStruct((1, vox), f32),),
        in_specs=[hbm, vmem, vmem, vmem, hbm, vmem],
        out_specs=(vmem,) * 5,
        scratch_shapes=[
            pltpu.VMEM((count, feat, cols), jnp.bfloat16),
            pltpu.VMEM((count, 2 * cols // LANES, LANES), jnp.bfloat16),
            pltpu.VMEM((count, 2 * cols // LANES, LANES), jnp.bfloat16),
            pltpu.VMEM((count * cols // LANES, LANES), f32),
            pltpu.VMEM((bricks, feat, vox), f32),
            pltpu.VMEM((bricks * feat, LANES), f32),
            pltpu.VMEM((bricks * feat, LANES), f32),
            pltpu.VMEM((ITERS + 1, bricks, vox), f32),
            pltpu.VMEM((ITERS, bricks, LANES), f32),
            pltpu.VMEM((bricks, LANES), f32),
            pltpu.VMEM((bricks, LANES), f32),
            pltpu.VMEM((bricks, LANES), f32),
            pltpu.VMEM((bricks, LANES), f32),
            pltpu.VMEM((bricks, LANES), f32),
            pltpu.VMEM((ITERS, 2, BX, LANES), f32),
            pltpu.VMEM((ITERS, 4, 8, LANES), f32),
            pltpu.VMEM((1, LANES), f32),
            pltpu.VMEM((count, 1, LANES), f32),
            pltpu.SemaphoreType.DMA,
            pltpu.SemaphoreType.DMA((count,)),
            pltpu.SemaphoreType.DMA((count,)),
            pltpu.SemaphoreType.DMA((count,)),
            pltpu.SemaphoreType.DMA((count,)),
            pltpu.SemaphoreType.DMA((ITERS, 4)),
            pltpu.SemaphoreType.DMA((ITERS, 4)),
            pltpu.SemaphoreType.DMA((count,)),
            pltpu.SemaphoreType.DMA((count,)),
        ],
        compiler_params=pltpu.CompilerParams(collective_id=0, has_side_effects=True),
    )(
        point_feats,
        point_targets.reshape(-1, LANES),
        point_lists.T,
        brick_adjacency.T,
        voxel_feats,
        voxel_reg,
    )
    return answer + alpha * direction, res - alpha * image


def solution(mesh):
    placed = (
        P(None, ("gx", "gy")),
        P(("gx", "gy")),
        P(("gx", "gy"), None),
        P(("gx", "gy"), None),
        P(("gx", "gy"), None, None),
        P(("gx", "gy"), None),
    )
    return jax.shard_map(
        functools.partial(shards, mesh.shape["gx"], mesh.shape["gy"]),
        mesh=mesh,
        in_specs=placed,
        out_specs=(P(("gx", "gy"), None), P(("gx", "gy"), None)),
        check_vma=False,
    )
```
